128 devices in a mesh: rt: 8 (over x, core), ct: 16 (over z, y).
Axes of the slice: x: 4, y: 4, z: 4, core: 2. Of those that a mesh axis runs over, the one named last changes fastest.
Arguments:
- children: float32 [4096, 12288], P(('rt', 'ct')), may hold values from -6 to 6
- row_map: int32 [4096], replicated, may hold values from 0 to 4095, as said below
- column_map: int32 [2, 12288], replicated, may hold values from 0 to 16383, as said below
- staircase: int32 [2, 48], replicated, may hold values from 640 to 2048, as said below
Outputs:
- factor_rows: float32 [512, 16384], P(None, 'ct')
- basis: float32 [512, 4096], P(None, 'rt')
- remainder: float32 [4096, 16384], P('rt', 'ct')
The draws below stay inside these ranges and needn't reach their ends.
Inputs may be any that keep to these rules, and one draw needn't show every extreme that they name: `row_map`: A permutation of the front rows. Of the 32 stacked child rows in each aligned block of 32 (the rows of one device), at most 8 have front rows in any one aligned block of 512 front rows, and every such block of child rows reaches 8 for some block of front rows. `column_map`: each row is strictly increasing, begins with 0, 1, ..., 511 and ends with 16383. `staircase`: each row is nondecreasing and ends with 2048.
All inputs are finite; a program needn't handle non-finite values.
Results may differ from the reference program's by a relative error of at most 0.0003.
Values sent between devices are 32-bit elements; how exact they have to be, the bound alone decides.
A program may use at most 128 MiB of HBM per device.

```python
import jax
import jax.numpy as jnp
from jax import lax

FRONT_COLS = 16384
TILE = 256
CHILD_COLS = 12288
PANEL = 512
FRONT_ROWS = 4096
CHILD_ROWS = 2048
SRC_ROWS = 32
CAP = 8
N_RT = 8
N_CT = 16


def shuffle_one(subkey):
    return jax.random.permutation(subkey, SRC_ROWS)


def draw_row_map(key, part):
    sources = N_RT * N_CT
    subkeys = jax.random.split(jax.random.fold_in(key, 101), 3)
    shifts = jax.random.permutation(subkeys[0], sources) % N_RT
    places = jnp.arange(SRC_ROWS, dtype=jnp.int32)
    offsets = jnp.where(places < CAP, 0, (places - CAP) % (N_RT - 1) + 1)
    targets = (shifts[:, None] + offsets[None, :]) % N_RT
    shuffles = jax.vmap(shuffle_one)(jax.random.split(subkeys[1], sources))
    targets = jnp.take_along_axis(targets, shuffles, axis=1).reshape(-1)
    ordering = jax.random.permutation(subkeys[2], FRONT_ROWS)
    grouped = ordering[jnp.argsort(targets[ordering], stable=True)]
    return jnp.zeros((FRONT_ROWS,), jnp.int32).at[grouped].set(jnp.arange(FRONT_ROWS, dtype=jnp.int32))


def one_child(subkey):
    picked = jax.random.permutation(subkey, FRONT_COLS - PANEL - 1)[:CHILD_COLS - PANEL - 1] + PANEL
    return jnp.concatenate([jnp.arange(PANEL, dtype=jnp.int32), jnp.sort(picked).astype(jnp.int32), jnp.full((1,), FRONT_COLS - 1, jnp.int32)])


def draw_column_map(key, part):
    return jax.vmap(one_child)(jax.random.split(jax.random.fold_in(key, 202), 2))


def draw_staircase(key, part):
    tile_count = CHILD_COLS // TILE
    increments = jax.random.randint(jax.random.fold_in(key, 303), (2, tile_count), TILE // 2, 2 * TILE + 1)
    counts = jnp.minimum(PANEL + jnp.cumsum(increments, axis=1), CHILD_ROWS)
    return counts.at[:, tile_count - 1].set(CHILD_ROWS).astype(jnp.int32)


def levels(stream_key, extent, cuts, smallest, largest):
    loudness, own = 1.0, jax.random.fold_in(stream_key, 6)
    for dim, blocks in cuts:
        heights = jnp.exp(jax.random.uniform(jax.random.fold_in(own, dim), (blocks,), jnp.float32, smallest / len(cuts), largest / len(cuts)))
        loudness = loudness * jnp.repeat(heights, extent[dim] // blocks).reshape([-1 if axis == dim else 1 for axis in range(len(extent))])
    return loudness


def gaussian(key, extent, scale, limit, cuts=(), held_as=jnp.bfloat16):
    array = scale * jax.random.normal(key, extent, jnp.float32)
    if cuts:
        array = array * levels(key, extent, cuts, -0.22, 0.18)
    return jnp.clip(array, -limit, limit).astype(held_as)


def setup_inputs(seed: int = 0) -> dict:
    keys = jax.random.split(jax.random.key(seed), 5)
    return {
        "children": gaussian(keys[0], (FRONT_ROWS, CHILD_COLS), 1.0, 6.0, ((0, 128),), jnp.float32),
        "row_map": draw_row_map(jax.random.fold_in(keys[4], 71), 0),
        "column_map": draw_column_map(jax.random.fold_in(keys[4], 71), 0),
        "staircase": draw_staircase(jax.random.fold_in(keys[4], 71), 0),
    }


def householder_upper(panel_cols):
    height = panel_cols.shape[0]
    panel_width = panel_cols.shape[1]
    row_ids = jnp.arange(height, dtype=jnp.int32)

    def reflect(column_index, work_block):
        column = lax.dynamic_index_in_dim(work_block, column_index, 1, keepdims=False)
        column = jnp.where(row_ids >= column_index, column, jnp.zeros_like(column))
        pivot = lax.dynamic_index_in_dim(column, column_index, 0, keepdims=False)
        length = jnp.sqrt(jnp.sum(column * column))
        signed = jnp.where(pivot >= 0, length, -length)
        vector = column + jnp.where(row_ids == column_index, signed, jnp.zeros_like(signed))
        factor = 2.0 / jnp.sum(vector * vector)
        product = jnp.dot(vector, work_block, precision=lax.Precision.HIGHEST)
        return work_block - factor * vector[:, None] * product[None, :]
    work_block = lax.fori_loop(0, panel_width, reflect, panel_cols)
    upper_part = jnp.triu(work_block[:panel_width])
    flips = jnp.where(jnp.diagonal(upper_part) >= 0, 1.0, -1.0).astype(panel_cols.dtype)
    return upper_part * flips[:, None]

def assemble(children, row_map, column_map, staircase):
    total_rows = row_map.shape[0]
    child_rows = total_rows // 2
    within_child = jnp.arange(child_rows, dtype=jnp.int32)
    front_block = jnp.zeros((total_rows, FRONT_COLS), children.dtype)
    for which_child in range(2):
        lower_row = which_child * child_rows
        child_block = children[lower_row:lower_row + child_rows]
        limits = jnp.repeat(staircase[which_child], TILE, total_repeat_length=CHILD_COLS)
        child_block = jnp.where(within_child[:, None] < limits[None, :], child_block, jnp.zeros_like(child_block))
        widened = jnp.zeros((child_rows, FRONT_COLS), children.dtype).at[:, column_map[which_child]].set(child_block)
        front_block = front_block.at[row_map[lower_row:lower_row + child_rows]].set(widened)
    return front_block

def reference(children, row_map, column_map, staircase):
    front_block = assemble(children, row_map, column_map, staircase)
    panel_cols = front_block[:, :PANEL]
    upper_part = householder_upper(panel_cols)
    basis = jax.scipy.linalg.solve_triangular(upper_part.T, panel_cols.T, lower=True)
    factor_rows = jnp.dot(basis, front_block, precision=lax.Precision.HIGHEST)
    removed = lax.dot_general(basis, factor_rows, (((0,), (0,)), ((), ())), precision=lax.Precision.HIGHEST)
    return (factor_rows, basis, front_block - removed)
```

```python
import functools

import jax
import jax.numpy as jnp
from jax import lax
from jax.experimental import pallas as pl
from jax.experimental.pallas import tpu as pltpu
from jax.sharding import PartitionSpec as P

TILE = 256
PANEL = 512
LANES = 128
NR = 8
NC = 16
SRC = 32
CAP = 8
ROWS_DEV = 512
BLOCK_COLS = 1024
FRONT_COLS = NC * BLOCK_COLS
FRONT_BLOCKS = FRONT_COLS // LANES

highest = lax.Precision.HIGHEST
high = lax.Precision.HIGH
f32 = jnp.float32
bf16 = jnp.bfloat16
MESH = pl.DeviceIdType.MESH


def place_kernel(q_ref, lim_ref, ch_ref, code_ref, sel_ref, out_ref, panel_ref):
    step = pl.program_id(0)
    row_ids = lax.broadcasted_iota(jnp.int32, (SRC, LANES), 0)
    sel = sel_ref[...]
    per_step = BLOCK_COLS // LANES
    for sub in range(per_step):
        b = step * per_step + sub
        q = q_ref[b]
        start = pl.multiple_of(q * LANES, LANES)
        v0 = ch_ref[:, pl.ds(start, LANES)]
        v1 = ch_ref[:, pl.ds(pl.multiple_of(start + LANES, LANES), LANES)]
        v0 = jnp.where(row_ids < lim_ref[q], v0, 0.0)
        v1 = jnp.where(row_ids < lim_ref[q + 1], v1, 0.0)
        code = jnp.broadcast_to(code_ref[pl.ds(b, 1), :], (SRC, LANES))
        lane = jnp.bitwise_and(code, LANES - 1)
        g0 = jnp.take_along_axis(v0, lane, axis=1)
        g1 = jnp.take_along_axis(v1, lane, axis=1)
        x = jnp.where(code < 0, 0.0, jnp.where(code < LANES, g0, g1))
        hi = x.astype(bf16)
        rest = x - hi.astype(f32)
        mid = rest.astype(bf16)
        low = (rest - mid.astype(f32)).astype(bf16)
        parts = jnp.concatenate([hi, mid, low], axis=0)
        y = jnp.dot(sel, parts, preferred_element_type=f32)
        y = y.reshape(NR, CAP, LANES)
        out_ref[:, 0, :, sub * LANES : (sub + 1) * LANES] = y
        if sub < PANEL // LANES:

            @pl.when(step == 0)
            def _():
                panel_ref[:, :, sub * LANES : (sub + 1) * LANES] = y


def place(children, code, q, lim, sel):
    child_cols = children.shape[1]
    return pl.pallas_call(
        place_kernel,
        grid_spec=pltpu.PrefetchScalarGridSpec(
            num_scalar_prefetch=2,
            grid=(NC,),
            in_specs=[
                pl.BlockSpec((SRC, child_cols), lambda i, *_: (0, 0)),
                pl.BlockSpec((FRONT_BLOCKS, LANES), lambda i, *_: (0, 0)),
                pl.BlockSpec((NR * CAP, 3 * SRC), lambda i, *_: (0, 0)),
            ],
            out_specs=[
                pl.BlockSpec((NR, 1, CAP, BLOCK_COLS), lambda i, *_: (0, i, 0, 0)),
                pl.BlockSpec((NR, CAP, PANEL), lambda i, *_: (0, 0, 0)),
            ],
        ),
        out_shape=[
            jax.ShapeDtypeStruct((NR, NC, CAP, BLOCK_COLS), f32),
            jax.ShapeDtypeStruct((NR, CAP, PANEL), f32),
        ],
        cost_estimate=pl.CostEstimate(flops=400_000_000, bytes_accessed=6_000_000, transcendentals=0),
    )(q, lim, children, code, sel)


def panel_kernel(
    po_ref, a_ref, g_ref, chunk, abuf, gpart, gin, gsum, gbuf, s1, r1, s2, r2, s3, r3, s4, r4
):
    r = lax.axis_index("rt")
    c = lax.axis_index("ct")
    barrier = pltpu.get_barrier_semaphore()
    for d in range(1, NR):
        pl.semaphore_signal(barrier, inc=1, device_id=(lax.rem(r + d, NR), c), device_id_type=MESH)
    for e in range(1, NC):
        pl.semaphore_signal(barrier, inc=1, device_id=(r, lax.rem(c + e, NC)), device_id_type=MESH)
    pl.semaphore_wait(barrier, NR + NC - 2)

    def to_rt(src_of, dst, send, recv):
        copies = []
        for d in range(1, NR):
            t = lax.rem(r + d, NR)
            copy = pltpu.make_async_remote_copy(
                src_ref=src_of(t),
                dst_ref=dst,
                send_sem=send.at[d - 1],
                recv_sem=recv.at[d - 1],
                device_id=(t, c),
                device_id_type=MESH,
            )
            copy.start()
            copies.append(copy)
        return copies

    def to_ct(src, dst, send, recv):
        copies = []
        for e in range(1, NC):
            copy = pltpu.make_async_remote_copy(
                src_ref=src,
                dst_ref=dst,
                send_sem=send.at[e - 1],
                recv_sem=recv.at[e - 1],
                device_id=(r, lax.rem(c + e, NC)),
                device_id_type=MESH,
            )
            copy.start()
            copies.append(copy)
        return copies

    copies = to_rt(lambda t: po_ref.at[t], chunk.at[r], s1, r1)
    chunk[r] = po_ref[r]
    for copy in copies:
        copy.wait()
    copies = to_ct(chunk, abuf.at[:, c], s2, r2)
    abuf[:, c] = chunk[...]
    for copy in copies:
        copy.wait()
    whole = abuf[...].reshape(NR * NC * CAP, PANEL)
    a_ref[...] = whole

    def gram_rows(i, carry):
        cols = a_ref[:, pl.ds(pl.multiple_of(i * LANES, LANES), LANES)]
        rows = lax.dot_general(
            cols.T, a_ref[...], (((1,), (0,)), ((), ())), precision=highest, preferred_element_type=f32
        )
        per = LANES // SRC
        gpart[pl.ds(i * per, per)] = rows.reshape(per, SRC, PANEL)
        return carry

    lax.fori_loop(0, PANEL // LANES, gram_rows, 0)
    copies = to_rt(lambda t: gpart.at[c], gin.at[r], s3, r3)
    gin[r] = gpart[c]
    for copy in copies:
        copy.wait()
    total = gin[0]
    for t in range(1, NR):
        total = total + gin[t]
    gsum[...] = total
    copies = to_ct(gsum, gbuf.at[c], s4, r4)
    gbuf[c] = total
    for copy in copies:
        copy.wait()
    g_ref[...] = gbuf[...].reshape(PANEL, PANEL)


def gather_panel(panel_out):
    slots = NR * NC * CAP
    dma = pltpu.SemaphoreType.DMA
    return pl.pallas_call(
        panel_kernel,
        in_specs=[pl.BlockSpec(memory_space=pltpu.VMEM)],
        out_specs=[pl.BlockSpec(memory_space=pltpu.VMEM)] * 2,
        out_shape=[
            jax.ShapeDtypeStruct((slots, PANEL), f32),
            jax.ShapeDtypeStruct((PANEL, PANEL), f32),
        ],
        scratch_shapes=[
            pltpu.VMEM((NR, CAP, PANEL), f32),
            pltpu.VMEM((NR, NC, CAP, PANEL), f32),
            pltpu.VMEM((NC, SRC, PANEL), f32),
            pltpu.VMEM((NR, SRC, PANEL), f32),
            pltpu.VMEM((SRC, PANEL), f32),
            pltpu.VMEM((NC, SRC, PANEL), f32),
            dma((NR - 1,)),
            dma((NR - 1,)),
            dma((NC - 1,)),
            dma((NC - 1,)),
            dma((NR - 1,)),
            dma((NR - 1,)),
            dma((NC - 1,)),
            dma((NC - 1,)),
        ],
        compiler_params=pltpu.CompilerParams(collective_id=0, has_side_effects=True),
        cost_estimate=pl.CostEstimate(flops=600_000_000, bytes_accessed=100_000_000, transcendentals=0),
    )(panel_out)


def sum_kernel(p_ref, out_ref, ain, half, bin_ref, mine, full, sa, ra, sb, rb, sc, rc, sd, rd):
    r = lax.axis_index("rt")
    c = lax.axis_index("ct")
    core = lax.rem(r, 2)
    x = r // 2
    sibling = r + 1 - 2 * core
    chips = NR // 2
    barrier = pltpu.get_barrier_semaphore()
    pl.semaphore_signal(barrier, inc=1, device_id=(sibling, c), device_id_type=MESH)
    peers = [2 * lax.rem(x + d, chips) + core for d in range(1, chips)]
    for peer in peers:
        pl.semaphore_signal(barrier, inc=1, device_id=(peer, c), device_id_type=MESH)
    pl.semaphore_wait(barrier, chips)

    def send(src, dst, ss, rs, to):
        copy = pltpu.make_async_remote_copy(
            src_ref=src, dst_ref=dst, send_sem=ss, recv_sem=rs, device_id=(to, c), device_id_type=MESH
        )
        copy.start()
        return copy

    swap = send(p_ref.at[1 - core], ain, sa, ra, sibling)
    swap.wait()
    half[...] = p_ref[core] + ain[...]
    copies = [
        send(half.at[peer // 2], bin_ref.at[d], sb.at[d], rb.at[d], peer)
        for d, peer in enumerate(peers)
    ]
    for copy in copies:
        copy.wait()
    mine[...] = (half[x] + bin_ref[0]) + (bin_ref[1] + bin_ref[2])
    copies = [
        send(mine, full.at[core, x], sc.at[d], rc.at[d], peer) for d, peer in enumerate(peers)
    ]
    last = [send(mine, full.at[core, x], sd.at[chips - 1], rd.at[chips - 1], sibling)]
    full[core, x] = mine[...]
    for d, copy in enumerate(copies):
        copy.wait()
        owner = lax.rem(x + chips - d - 1, chips)
        last.append(
            send(full.at[core, owner], full.at[core, owner], sd.at[d], rd.at[d], sibling)
        )
    for copy in last:
        copy.wait()
    out_ref[...] = full[...].reshape(out_ref.shape)


def sum_over_rt(part):
    rows, cols = part.shape
    chips = NR // 2
    sl = rows // NR
    dma = pltpu.SemaphoreType.DMA
    return pl.pallas_call(
        sum_kernel,
        in_specs=[pl.BlockSpec(memory_space=pltpu.VMEM)],
        out_specs=pl.BlockSpec(memory_space=pltpu.VMEM),
        out_shape=jax.ShapeDtypeStruct((rows, cols), f32),
        scratch_shapes=[
            pltpu.VMEM((chips, sl, cols), f32),
            pltpu.VMEM((chips, sl, cols), f32),
            pltpu.VMEM((chips - 1, sl, cols), f32),
            pltpu.VMEM((sl, cols), f32),
            pltpu.VMEM((2, chips, sl, cols), f32),
            dma(()),
            dma(()),
            dma((chips - 1,)),
            dma((chips - 1,)),
            dma((chips - 1,)),
            dma((chips - 1,)),
            dma((chips,)),
            dma((chips,)),
        ],
        compiler_params=pltpu.CompilerParams(collective_id=1, has_side_effects=True),
        cost_estimate=pl.CostEstimate(flops=1_000_000, bytes_accessed=100_000_000, transcendentals=0),
    )(part.reshape(2, chips, sl, cols))


def tables(row_map, column_map, staircase, r, c):
    sources = NR * NC
    device_id = r * NC + c
    which_child = r // (NR // 2)
    tile = (row_map // ROWS_DEV).reshape(sources, SRC)
    same = tile[:, :, None] == tile[:, None, :]
    before = jnp.arange(SRC)[:, None] > jnp.arange(SRC)[None, :]
    rank = jnp.sum((same & before[None]).astype(jnp.int32), axis=2)
    my_slot = lax.dynamic_index_in_dim(tile * CAP + rank, device_id, 0, keepdims=False)
    select = my_slot[None, :] == jnp.arange(NR * CAP, dtype=jnp.int32)[:, None]
    select = jnp.tile(select.astype(bf16), (1, 3))
    local = row_map.reshape(sources, SRC) - r * ROWS_DEV
    hit = (tile == r)[:, :, None] & (rank[:, :, None] == jnp.arange(CAP)[None, None, :])
    front_of_slot = jnp.sum(jnp.where(hit, local[:, :, None] + 1, 0), axis=1).reshape(-1) - 1
    slot_of_front = jnp.sum(
        jnp.where(
            front_of_slot[None, :] == jnp.arange(ROWS_DEV, dtype=jnp.int32)[:, None],
            jnp.arange(sources * CAP, dtype=jnp.int32)[None, :],
            0,
        ),
        axis=1,
    )
    cmap = lax.dynamic_index_in_dim(column_map, which_child, 0, keepdims=False)
    stair = lax.dynamic_index_in_dim(staircase, which_child, 0, keepdims=False)
    blocks = jnp.arange(FRONT_BLOCKS, dtype=jnp.int32)
    high_part = ((cmap // LANES)[None, :] == blocks[:, None]).astype(bf16)
    low_part = ((cmap % LANES)[None, :] == jnp.arange(LANES, dtype=jnp.int32)[:, None]).astype(bf16)
    present = lax.dot_general(high_part, low_part, (((1,), (1,)), ((), ())), preferred_element_type=f32)
    upper = (jnp.arange(LANES)[:, None] < jnp.arange(LANES)[None, :]).astype(bf16)
    inside = jnp.dot(present.astype(bf16), upper, preferred_element_type=f32)
    counts = jnp.sum(present, axis=1)
    starts = jnp.sum(jnp.where(blocks[None, :] < blocks[:, None], counts[None, :], 0.0), axis=1)
    starts = starts.astype(jnp.int32)
    child_blocks = cmap.shape[0] // LANES
    q = jnp.minimum(starts // LANES, child_blocks - 2)
    code = starts[:, None] + inside.astype(jnp.int32) - q[:, None] * LANES
    code = jnp.where(present > 0.5, code, -1)
    first = lax.rem(device_id * SRC, row_map.shape[0] // 2)
    lim = jnp.repeat(stair, TILE // LANES, total_repeat_length=child_blocks) - first
    return select, slot_of_front, code, q, lim


def shards(children, row_map, column_map, staircase):
    r = lax.axis_index("rt")
    c = lax.axis_index("ct")
    select, slot_of_front, code, q, lim = tables(row_map, column_map, staircase, r, c)
    outgoing, panel_out = place(children, code, q, lim, select)
    arrived = lax.all_to_all(
        outgoing.reshape(NR * NC, CAP, BLOCK_COLS),
        ("rt", "ct"),
        split_axis=0,
        concat_axis=0,
        tiled=True,
    )
    panel_rows, gram = gather_panel(panel_out)
    lower = jnp.linalg.cholesky(gram)
    inverse = jax.scipy.linalg.solve_triangular(lower, jnp.eye(PANEL, dtype=f32), lower=True)
    arrived = arrived.reshape(NR * NC * CAP, BLOCK_COLS)
    part = lax.dot_general(
        panel_rows, arrived, (((0,), (0,)), ((), ())), precision=high, preferred_element_type=f32
    )
    projected = sum_over_rt(part)
    front_block = arrived[slot_of_front]
    panel_block = panel_rows[slot_of_front]
    basis = lax.dot_general(
        inverse, panel_block, (((1,), (1,)), ((), ())), precision=high, preferred_element_type=f32
    )
    factor_rows = jnp.dot(inverse, projected, precision=high, preferred_element_type=f32)
    update = lax.dot_general(
        basis, factor_rows, (((0,), (0,)), ((), ())), precision=high, preferred_element_type=f32
    )
    return (factor_rows, basis, front_block - update)


def solution(mesh):
    placed = (P(("rt", "ct"), None), P(), P(), P())
    return jax.shard_map(
        shards,
        mesh=mesh,
        in_specs=placed,
        out_specs=(P(None, "ct"), P(None, "rt"), P("rt", "ct")),
        check_vma=False,
    )
```

```python
import functools

import jax
import jax.numpy as jnp
from jax import lax
from jax.experimental import pallas as pl
from jax.experimental.pallas import tpu as pltpu
from jax.sharding import PartitionSpec as P

TILE = 256
PANEL = 512
SUB = 8
LANES = 128
NR = 8
NC = 16
SRC = 32
CAP = 8
ROWS_DEV = 512
BLOCK_COLS = 1024
FRONT_COLS = NC * BLOCK_COLS
FRONT_BLOCKS = FRONT_COLS // LANES
QUARTERS = 4
QCOLS = BLOCK_COLS // QUARTERS
SIDE = 4
CHIPS = NR // 2
SLICE = PANEL // NR
PAIRS = [(i, j) for i in range(PANEL // LANES) for j in range(i, PANEL // LANES)]

highest = lax.Precision.HIGHEST
high = lax.Precision.HIGH
f32 = jnp.float32
bf16 = jnp.bfloat16
MESH = pl.DeviceIdType.MESH


def place_kernel(q_ref, lim_ref, ch_ref, code_ref, out_ref, panel_ref):
    step = pl.program_id(0)
    row_ids = lax.broadcasted_iota(jnp.int32, (SUB, LANES), 0)
    per_step = BLOCK_COLS // LANES
    for sub in range(per_step):
        b = step * per_step + sub
        q = q_ref[b]
        start = pl.multiple_of(q * LANES, LANES)
        after = pl.multiple_of(start + LANES, LANES)
        code = jnp.broadcast_to(code_ref[pl.ds(b, 1), :], (SUB, LANES))
        lane = jnp.bitwise_and(code, LANES - 1)
        first = lim_ref[q]
        second = lim_ref[q + 1]
        limit = jnp.where(code < LANES, first, second)
        limit = jnp.where(code < 0, 0, limit)
        quarter, offset = divmod(sub * LANES, QCOLS)
        for g in range(SRC // SUB):
            v0 = ch_ref[g * SUB : (g + 1) * SUB, pl.ds(start, LANES)]
            v1 = ch_ref[g * SUB : (g + 1) * SUB, pl.ds(after, LANES)]
            g0 = jnp.take_along_axis(v0, lane, axis=1)
            g1 = jnp.take_along_axis(v1, lane, axis=1)
            x = jnp.where(code < LANES, g0, g1)
            x = jnp.where(row_ids + g * SUB < limit, x, 0.0)
            out_ref[quarter, 0, g * SUB : (g + 1) * SUB, offset : offset + LANES] = x
            if sub < PANEL // LANES:

                @pl.when(step == 0)
                def _():
                    panel_ref[g * SUB : (g + 1) * SUB, sub * LANES : (sub + 1) * LANES] = x


def place(children, code, q, lim):
    child_cols = children.shape[1]
    return pl.pallas_call(
        place_kernel,
        grid_spec=pltpu.PrefetchScalarGridSpec(
            num_scalar_prefetch=2,
            grid=(NC,),
            in_specs=[
                pl.BlockSpec((SRC, child_cols), lambda i, *_: (0, 0)),
                pl.BlockSpec((FRONT_BLOCKS, LANES), lambda i, *_: (0, 0)),
            ],
            out_specs=[
                pl.BlockSpec((QUARTERS, 1, SRC, QCOLS), lambda i, *_: (0, i, 0, 0)),
                pl.BlockSpec((SRC, PANEL), lambda i, *_: (0, 0)),
            ],
        ),
        out_shape=[
            jax.ShapeDtypeStruct((QUARTERS, NC, SRC, QCOLS), f32),
            jax.ShapeDtypeStruct((SRC, PANEL), f32),
        ],
        cost_estimate=pl.CostEstimate(flops=10_000_000, bytes_accessed=4_000_000, transcendentals=0),
    )(q, lim, children, code)


def across_lanes(v, lane):
    return jnp.broadcast_to(v[:, lane : lane + 1], (SUB, LANES))

def across_rows(v, row):
    return jnp.broadcast_to(v[row : row + 1, :], (SUB, LANES))

def inverse_of_block(block, unit, write):
    groups = LANES // SUB
    sub = lax.broadcasted_iota(jnp.int32, (SUB, LANES), 0)
    for g in range(groups):
        cols = [across_lanes(block[g], SUB * g + m) for m in range(SUB)]
        a = {(i, m): across_rows(cols[m], i) for m in range(SUB) for i in range(m, SUB)}
        low = {}
        inv = {}
        for k in range(SUB):
            inv[k, k] = lax.rsqrt(a[k, k])
            for i in range(k + 1, SUB):
                low[i, k] = a[i, k] * inv[k, k]
            for i in range(k + 1, SUB):
                for m in range(k + 1, i + 1):
                    a[i, m] = a[i, m] - low[i, k] * low[m, k]
        for i in range(1, SUB):
            for k in range(i):
                acc = low[i, k] * inv[k, k]
                for m in range(k + 1, i):
                    acc = acc + low[i, m] * inv[m, k]
                inv[i, k] = -inv[i, i] * acc
        zero = jnp.zeros((SUB, LANES), f32)
        down = []
        for k in range(SUB):
            col = zero
            for i in range(k, SUB):
                col = jnp.where(sub == i, inv[i, k], col)
            down.append(col)
        up = []
        for k in range(SUB):
            col = zero
            for i in range(k + 1):
                col = jnp.where(sub == i, inv[k, i], col)
            up.append(col)

        def apply(cols, v):
            terms = [cols[k] * across_rows(v, k) for k in range(SUB)]
            while len(terms) > 1:
                terms = [terms[i] + terms[i + 1] for i in range(0, len(terms), 2)]
            return terms[0]

        done = apply(down, unit[g])
        write(g, done)
        if g + 1 < groups:
            z = apply(up, apply(down, block[g]))
            zu = apply(up, done)
            zr = [across_rows(z, m) for m in range(SUB)]
            zur = [across_rows(zu, m) for m in range(SUB)]
            for i in range(g + 1, groups):
                mult = [across_lanes(block[i], SUB * g + m) for m in range(SUB)]
                t = [mult[m] * zr[m] for m in range(SUB)]
                u = [mult[m] * zur[m] for m in range(SUB)]
                while len(t) > 1:
                    t = [t[j] + t[j + 1] for j in range(0, len(t), 2)]
                    u = [u[j] + u[j + 1] for j in range(0, len(u), 2)]
                block[i] = block[i] - t[0]
                unit[i] = unit[i] - u[0]


def three_parts(x):
    hi = x.astype(bf16)
    rest = x - hi.astype(f32)
    mid = rest.astype(bf16)
    low = (rest - mid.astype(f32)).astype(bf16)
    return jnp.concatenate([hi, mid, low], axis=0)


def two_parts(x):
    hi = x.astype(bf16)
    return hi, (x - hi.astype(f32)).astype(bf16)


class GatherCt:
    def __init__(self, source, dest, r, c, s1, r1, s2, r2):
        self.source, self.dest, self.r, self.c = source, dest, r, c
        self.sems = (s1, r1, s2, r2)
        self.first, self.second = [], []

    def along(self, half, d):
        z, y = self.c // SIDE, lax.rem(self.c, SIDE)
        if half == 0:
            return z * SIDE + lax.rem(y + d, SIDE)
        return lax.rem(z + d, SIDE) * SIDE + y

    def send(self, src, half, owner, to, ss, rs):
        copy = pltpu.make_async_remote_copy(
            src_ref=src,
            dst_ref=self.dest(half, owner),
            send_sem=ss,
            recv_sem=rs,
            device_id=(self.r, to),
            device_id_type=MESH,
        )
        copy.start()
        return copy

    def start(self):
        s1, r1, s2, r2 = self.sems
        for d in range(1, SIDE):
            for h in range(2):
                to = self.along(h, d)
                copy = self.send(self.source(h), h, self.c, to, s1.at[h, d - 1], r1.at[h, d - 1])
                self.first.append(copy)
        for d in range(1, SIDE):
            for h in range(2):
                to = self.along(1 - h, d)
                copy = self.send(
                    self.source(h), h, self.c, to, s2.at[h, 0, d - 1], r2.at[h, 0, d - 1]
                )
                self.second.append(copy)

    def forward(self):
        s1, r1, s2, r2 = self.sems
        position = 0
        for p in range(1, SIDE):
            for h in range(2):
                self.first[position].wait()
                position += 1
                owner = self.along(h, SIDE - p)
                for d in range(1, SIDE):
                    to = self.along(1 - h, d)
                    copy = self.send(
                        self.dest(h, owner), h, owner, to, s2.at[h, p, d - 1], r2.at[h, p, d - 1]
                    )
                    self.second.append(copy)

    def finish(self):
        for copy in self.second:
            copy.wait()


def front_kernel(
    x_ref, pan_ref, sel_ref, fs_ref, as_ref, sum_ref, inv_ref,
    po, chunk, ap, apt, gpart, gin, gsum, gbuf, fp, routed, work, small,
    part, ain, half, bin_ref, mine, full,
    p1s, p1r, a1s, a1r, a2s, a2r, c1s, c1r, c2s, c2r, g1s, g1r, g2s, g2r, p3s, p3r,
    t1s, t1r, t2s, t2r, sa, ra, sb, rb, sc, rc, sd, rd, own,
):
    r = lax.axis_index("rt")
    c = lax.axis_index("ct")
    core = lax.rem(r, 2)
    x = r // 2
    sibling = r + 1 - 2 * core
    chip_peers = [2 * lax.rem(x + d, CHIPS) + core for d in range(1, CHIPS)]
    barrier = pltpu.get_barrier_semaphore()
    for d in range(1, NR):
        pl.semaphore_signal(barrier, inc=1, device_id=(lax.rem(r + d, NR), c), device_id_type=MESH)
    for e in range(1, NC):
        pl.semaphore_signal(barrier, inc=1, device_id=(r, lax.rem(c + e, NC)), device_id_type=MESH)

    pieces = three_parts(pan_ref[...])
    po[...] = jnp.dot(sel_ref[c], pieces, preferred_element_type=f32).reshape(NR, CAP, PANEL)
    ap[c] = pan_ref[...]
    pl.semaphore_wait(barrier, NR + NC - 2)

    def send(src, dst, ss, rs, rt, ct):
        copy = pltpu.make_async_remote_copy(
            src_ref=src, dst_ref=dst, send_sem=ss, recv_sem=rs, device_id=(rt, ct), device_id_type=MESH
        )
        copy.start()
        return copy

    def to_rt(src_of, dst, ss, rs):
        copies = []
        for d in range(1, NR):
            t = lax.rem(r + d, NR)
            copies.append(send(src_of(t), dst, ss.at[d - 1], rs.at[d - 1], t, c))
        return copies

    def wait_all(copies):
        for copy in copies:
            copy.wait()

    def start_columns(j):
        copies = []
        for e in range(1, NC):
            to = lax.rem(c + e, NC)
            copies.append(
                send(x_ref.at[j, to], fp.at[j, c], t1s.at[j, e - 1], t1r.at[j, e - 1], r, to)
            )
        fp[j, c] = x_ref[j, c]
        return copies

    local = []

    def route(j, copies):
        wait_all(copies)

        def one(s, carry):
            y = jnp.dot(sel_ref[s], three_parts(fp[j, s]), preferred_element_type=f32)
            routed[j, :, pl.ds(pl.multiple_of(s * CAP, CAP), CAP), :] = y.reshape(NR, CAP, QCOLS)
            return carry

        lax.fori_loop(0, NC, one, 0)
        here = fs_ref.at[r, :, pl.ds(j * QCOLS, QCOLS)]
        sends = to_rt(lambda t: routed.at[j, t], here, t2s.at[j], t2r.at[j])
        keep = pltpu.make_async_copy(routed.at[j, r], here, own.at[j])
        keep.start()
        local.append(keep)
        return sends

    panel = GatherCt(
        lambda h: pan_ref.at[pl.ds(h * SRC // 2, SRC // 2)],
        lambda h, o: ap.at[o, pl.ds(h * SRC // 2, SRC // 2)],
        r, c, a1s, a1r, a2s, a2r,
    )
    rows = GatherCt(
        lambda h: chunk.at[pl.ds(h * NR // 2, NR // 2)],
        lambda h, o: as_ref.at[pl.ds(h * NR // 2, NR // 2), o],
        r, c, c1s, c1r, c2s, c2r,
    )
    grams = GatherCt(
        lambda h: gsum.at[pl.ds(h * len(PAIRS) // 2, len(PAIRS) // 2)],
        lambda h, o: gbuf.at[o, pl.ds(h * len(PAIRS) // 2, len(PAIRS) // 2)],
        r, c, g1s, g1r, g2s, g2r,
    )

    panel.start()
    chunks = to_rt(lambda t: po.at[t], chunk.at[r], p1s, p1r)
    chunk[r] = po[r]
    columns = [start_columns(0)]
    panel.forward()
    columns.append(start_columns(1))
    panel.finish()
    columns.append(start_columns(2))
    columns.append(start_columns(3))

    whole = ap[...].reshape(NC * SRC, PANEL)
    apt[...] = whole.T
    for i in range(PANEL // LANES):
        block = jnp.dot(
            apt[i * LANES : (i + 1) * LANES, :],
            ap[:, :, i * LANES :].reshape(NC * SRC, PANEL - i * LANES),
            precision=highest,
            preferred_element_type=f32,
        )
        for j in range(i, PANEL // LANES):
            piece = block[:, (j - i) * LANES : (j - i + 1) * LANES]
            gpart[:, PAIRS.index((i, j))] = piece.reshape(NC, SUB, LANES)
    gram_sends = to_rt(lambda t: gpart.at[c], gin.at[r], p3s, p3r)
    gin[r] = gpart[c]

    routes = [route(0, columns[0])]
    wait_all(gram_sends)
    total = gin[0]
    for t in range(1, NR):
        total = total + gin[t]
    gsum[...] = total
    grams.start()
    gbuf[c] = total
    routes.append(route(1, columns[1]))
    grams.forward()
    wait_all(chunks)
    rows.start()
    keep = pltpu.make_async_copy(chunk, as_ref.at[:, c], own.at[QUARTERS])
    keep.start()
    local.append(keep)
    routes.append(route(2, columns[2]))
    grams.finish()
    for n, (i, j) in enumerate(PAIRS):
        work[i * LANES : (i + 1) * LANES, j * LANES : (j + 1) * LANES] = gbuf[:, n].reshape(LANES, LANES)
    ids = lax.broadcasted_iota(jnp.int32, (PANEL, PANEL), 0)
    lanes = lax.broadcasted_iota(jnp.int32, (PANEL, PANEL), 1)
    work[:, PANEL:] = jnp.where(ids == lanes, 1.0, 0.0).astype(f32)
    routes.append(route(3, columns[3]))
    rows.forward()

    def product(n, carry):
        i = n // QUARTERS
        j = lax.rem(n, QUARTERS)
        ah, al = two_parts(apt[pl.ds(pl.multiple_of(i * LANES, LANES), LANES), :])
        bh, bl = two_parts(fp[j].reshape(NC * SRC, QCOLS))
        y = jnp.dot(ah, bh, preferred_element_type=f32)
        y = y + jnp.dot(ah, bl, preferred_element_type=f32)
        y = y + jnp.dot(al, bh, preferred_element_type=f32)
        y = y.reshape(LANES // SLICE, SLICE, QCOLS)
        at = pl.ds(lax.rem(i, 2) * (LANES // SLICE), LANES // SLICE)
        part[i // 2, at, :, pl.ds(pl.multiple_of(j * QCOLS, QCOLS), QCOLS)] = y
        return carry

    lax.fori_loop(0, QUARTERS * (PANEL // LANES), product, 0)
    swap = send(part.at[1 - core], ain, sa, ra, sibling, c)

    factor_step(0, work, small)
    swap.wait()
    half[...] = part[core] + ain[...]
    spread = [
        send(half.at[peer // 2], bin_ref.at[d], sb.at[d], rb.at[d], peer, c)
        for d, peer in enumerate(chip_peers)
    ]
    factor_step(1, work, small)
    factor_step(2, work, small)
    wait_all(spread)
    mine[...] = (half[x] + bin_ref[0]) + (bin_ref[1] + bin_ref[2])
    spread = [
        send(mine, full.at[core, x], sc.at[d], rc.at[d], peer, c) for d, peer in enumerate(chip_peers)
    ]
    last = [send(mine, full.at[core, x], sd.at[CHIPS - 1], rd.at[CHIPS - 1], sibling, c)]
    full[core, x] = mine[...]
    factor_step(3, work, small)
    inv_ref[...] = work[:, PANEL:]
    for d, copy in enumerate(spread):
        copy.wait()
        owner = lax.rem(x + CHIPS - d - 1, CHIPS)
        last.append(
            send(full.at[core, owner], full.at[core, owner], sd.at[d], rd.at[d], sibling, c)
        )
    rows.finish()
    wait_all(last)
    sum_ref[...] = full[...].reshape(PANEL, BLOCK_COLS)
    for copies in routes:
        wait_all(copies)
    wait_all(local)


def factor_step(b, work, small):
    o = b * LANES
    lane = lax.broadcasted_iota(jnp.int32, (SUB, LANES), 1)
    sub = lax.broadcasted_iota(jnp.int32, (SUB, LANES), 0)
    block = [work[o + SUB * g : o + SUB * (g + 1), o : o + LANES] for g in range(LANES // SUB)]
    unit = [jnp.where(lane == sub + SUB * g, 1.0, 0.0).astype(f32) for g in range(LANES // SUB)]

    def write(g, v):
        small[SUB * g : SUB * (g + 1), :] = v

    inverse_of_block(block, unit, write)
    end = PANEL + o + LANES
    row = jnp.dot(
        small[...], work[o : o + LANES, o:end], precision=highest, preferred_element_type=f32
    )
    work[o : o + LANES, o:end] = row
    for p in range(o + LANES, PANEL, LANES):
        mult = row[:, p - o : p - o + LANES]
        work[p : p + LANES, p:end] = work[p : p + LANES, p:end] - jnp.dot(
            mult.T, row[:, p - o :], precision=highest, preferred_element_type=f32
        )


def build_front(columns, panel, select):
    slots = NC * CAP
    vmem = pltpu.VMEM
    dma = pltpu.SemaphoreType.DMA
    n = len(PAIRS)
    ring = [dma((2, SIDE - 1)), dma((2, SIDE - 1)), dma((2, SIDE, SIDE - 1)), dma((2, SIDE, SIDE - 1))]
    return pl.pallas_call(
        front_kernel,
        in_specs=[pl.BlockSpec(memory_space=pltpu.VMEM)] * 3,
        out_specs=[pl.BlockSpec(memory_space=pl.ANY)] * 2 + [pl.BlockSpec(memory_space=pltpu.VMEM)] * 2,
        out_shape=[
            jax.ShapeDtypeStruct((NR, slots, BLOCK_COLS), f32),
            jax.ShapeDtypeStruct((NR, NC, CAP, PANEL), f32),
            jax.ShapeDtypeStruct((PANEL, BLOCK_COLS), f32),
            jax.ShapeDtypeStruct((PANEL, PANEL), f32),
        ],
        scratch_shapes=[
            vmem((NR, CAP, PANEL), f32),
            vmem((NR, CAP, PANEL), f32),
            vmem((NC, SRC, PANEL), f32),
            vmem((PANEL, NC * SRC), f32),
            vmem((NC, n, SUB, LANES), f32),
            vmem((NR, n, SUB, LANES), f32),
            vmem((n, SUB, LANES), f32),
            vmem((NC, n, SUB, LANES), f32),
            vmem((QUARTERS, NC, SRC, QCOLS), f32),
            vmem((QUARTERS, NR, slots, QCOLS), f32),
            vmem((PANEL, 2 * PANEL), f32),
            vmem((LANES, LANES), f32),
            vmem((2, CHIPS, SLICE, BLOCK_COLS), f32),
            vmem((CHIPS, SLICE, BLOCK_COLS), f32),
            vmem((CHIPS, SLICE, BLOCK_COLS), f32),
            vmem((CHIPS - 1, SLICE, BLOCK_COLS), f32),
            vmem((SLICE, BLOCK_COLS), f32),
            vmem((2, CHIPS, SLICE, BLOCK_COLS), f32),
            dma((NR - 1,)),
            dma((NR - 1,)),
            *ring,
            *ring,
            *ring,
            dma((NR - 1,)),
            dma((NR - 1,)),
            dma((QUARTERS, NC - 1)),
            dma((QUARTERS, NC - 1)),
            dma((QUARTERS, NR - 1)),
            dma((QUARTERS, NR - 1)),
            dma(()),
            dma(()),
            dma((CHIPS - 1,)),
            dma((CHIPS - 1,)),
            dma((CHIPS - 1,)),
            dma((CHIPS - 1,)),
            dma((CHIPS,)),
            dma((CHIPS,)),
            dma((QUARTERS + 1,)),
        ],
        compiler_params=pltpu.CompilerParams(collective_id=0, has_side_effects=True),
        cost_estimate=pl.CostEstimate(
            flops=3_000_000_000, bytes_accessed=300_000_000, transcendentals=0
        ),
    )(columns, panel, select)


def tables(row_map, column_map, staircase, r, c):
    sources = NR * NC
    device_id = r * NC + c
    which_child = r // (NR // 2)
    tile = (row_map // ROWS_DEV).reshape(sources, SRC)
    same = tile[:, :, None] == tile[:, None, :]
    before = jnp.arange(SRC)[:, None] > jnp.arange(SRC)[None, :]
    rank = jnp.sum((same & before[None]).astype(jnp.int32), axis=2)
    slots = lax.dynamic_slice_in_dim(tile * CAP + rank, r * NC, NC)
    select = slots[:, None, :] == jnp.arange(NR * CAP, dtype=jnp.int32)[None, :, None]
    select = jnp.tile(select.astype(bf16), (1, 1, 3))
    local = row_map.reshape(sources, SRC) - r * ROWS_DEV
    hit = (tile == r)[:, :, None] & (rank[:, :, None] == jnp.arange(CAP)[None, None, :])
    front_of_slot = jnp.sum(jnp.where(hit, local[:, :, None] + 1, 0), axis=1).reshape(-1) - 1
    slot_of_front = jnp.sum(
        jnp.where(
            front_of_slot[None, :] == jnp.arange(ROWS_DEV, dtype=jnp.int32)[:, None],
            jnp.arange(sources * CAP, dtype=jnp.int32)[None, :],
            0,
        ),
        axis=1,
    )
    cmap = lax.dynamic_index_in_dim(column_map, which_child, 0, keepdims=False)
    stair = lax.dynamic_index_in_dim(staircase, which_child, 0, keepdims=False)
    blocks = jnp.arange(FRONT_BLOCKS, dtype=jnp.int32)
    high_part = ((cmap // LANES)[None, :] == blocks[:, None]).astype(bf16)
    low_part = ((cmap % LANES)[None, :] == jnp.arange(LANES, dtype=jnp.int32)[:, None]).astype(bf16)
    present = lax.dot_general(high_part, low_part, (((1,), (1,)), ((), ())), preferred_element_type=f32)
    upper = (jnp.arange(LANES)[:, None] < jnp.arange(LANES)[None, :]).astype(bf16)
    inside = jnp.dot(present.astype(bf16), upper, preferred_element_type=f32)
    counts = jnp.sum(present, axis=1)
    starts = jnp.sum(jnp.where(blocks[None, :] < blocks[:, None], counts[None, :], 0.0), axis=1)
    starts = starts.astype(jnp.int32)
    child_blocks = cmap.shape[0] // LANES
    q = jnp.minimum(starts // LANES, child_blocks - 2)
    code = starts[:, None] + inside.astype(jnp.int32) - q[:, None] * LANES
    code = jnp.where(present > 0.5, code, -1)
    first = lax.rem(device_id * SRC, row_map.shape[0] // 2)
    lim = jnp.repeat(stair, TILE // LANES, total_repeat_length=child_blocks) - first
    return select, slot_of_front, code, q, lim


def shards(children, row_map, column_map, staircase):
    r = lax.axis_index("rt")
    c = lax.axis_index("ct")
    select, slot_of_front, code, q, lim = tables(row_map, column_map, staircase, r, c)
    columns, panel = place(children, code, q, lim)
    arrived, panel_rows, projected, inverse = build_front(columns, panel, select)
    front_block = arrived.reshape(NR * NC * CAP, BLOCK_COLS)[slot_of_front]
    panel_block = panel_rows.reshape(NR * NC * CAP, PANEL)[slot_of_front]
    basis = lax.dot_general(
        inverse, panel_block, (((1,), (1,)), ((), ())), precision=high, preferred_element_type=f32
    )
    factor_rows = jnp.dot(inverse, projected, precision=high, preferred_element_type=f32)
    update = lax.dot_general(
        basis, factor_rows, (((0,), (0,)), ((), ())), precision=high, preferred_element_type=f32
    )
    return (factor_rows, basis, front_block - update)


def solution(mesh):
    placed = (P(("rt", "ct"), None), P(), P(), P())
    return jax.shard_map(
        shards,
        mesh=mesh,
        in_specs=placed,
        out_specs=(P(None, "ct"), P(None, "rt"), P("rt", "ct")),
        check_vma=False,
    )
```

```python
import functools

import jax
import jax.numpy as jnp
from jax import lax
from jax.experimental import pallas as pl
from jax.experimental.pallas import tpu as pltpu
from jax.sharding import PartitionSpec as P

TILE = 256
PANEL = 512
SUB = 8
LANES = 128
NR = 8
NC = 16
SRC = 32
CAP = 8
ROWS_DEV = 512
BLOCK_COLS = 1024
FRONT_COLS = NC * BLOCK_COLS
FRONT_BLOCKS = FRONT_COLS // LANES
QUARTERS = 4
QCOLS = BLOCK_COLS // QUARTERS
SIDE = 4
CHIPS = NR // 2
SLICE = PANEL // NR
PAIRS = [(i, j) for i in range(PANEL // LANES) for j in range(i, PANEL // LANES)]

highest = lax.Precision.HIGHEST
high = lax.Precision.HIGH
f32 = jnp.float32
bf16 = jnp.bfloat16
MESH = pl.DeviceIdType.MESH


def table_kernel(
    stair_ref, row_ref, col_ref, ch_ref, x_ref, pan_ref, slot_ref, front_ref, code_ref, qv_ref, q_ref, sem
):
    r = lax.axis_index("rt")
    c = lax.axis_index("ct")
    child = r // (NR // 2)
    child_cols = col_ref.shape[1]
    rows = row_ref.shape[0]
    sub = lax.broadcasted_iota(jnp.int32, (LANES, LANES), 0)
    lane = lax.broadcasted_iota(jnp.int32, (LANES, LANES), 1)

    step = child_cols // 6
    ids = lax.broadcasted_iota(jnp.int32, (LANES, step), 0)
    present = jnp.zeros((LANES, LANES), f32)
    for n in range(6):
        cm = col_ref[pl.ds(child, 1), n * step : (n + 1) * step]
        cm = jnp.broadcast_to(cm, (LANES, step))
        upper = (jnp.right_shift(cm, 7) == ids).astype(f32).astype(bf16)
        lower = (jnp.bitwise_and(cm, LANES - 1) == ids).astype(f32).astype(bf16)
        present = present + lax.dot_general(
            upper, lower, (((1,), (1,)), ((), ())), preferred_element_type=f32
        )
    flags = present.astype(bf16)
    before = (sub < lane).astype(f32).astype(bf16)
    inside = jnp.dot(flags, before, preferred_element_type=f32)
    above = jnp.dot((lane < sub).astype(f32).astype(bf16), flags, preferred_element_type=f32)
    starts = jnp.sum(above, axis=1, keepdims=True).astype(jnp.int32)
    last = child_cols // LANES - 2
    q = jnp.minimum(jnp.right_shift(starts, 7), last)
    code = starts - q * LANES + inside.astype(jnp.int32)
    code_ref[...] = jnp.where(present > 0.5, code, -1)
    across = lax.dot_general(
        jnp.ones((SUB, LANES), bf16), above.astype(bf16), (((1,), (1,)), ((), ())),
        preferred_element_type=f32,
    )
    qv_ref[...] = jnp.minimum(jnp.right_shift(across.astype(jnp.int32), 7), last)

    rm = row_ref[...]
    tile = jnp.right_shift(rm, 9)
    group = jnp.right_shift(sub, 5) == jnp.right_shift(lane, 5)
    earlier = (group & (sub < lane)).astype(f32).astype(bf16)
    slot = jnp.zeros((rows, LANES), jnp.int32)
    for t in range(NR):
        hit = tile == t
        rank = jnp.dot(hit.astype(f32).astype(bf16), earlier, preferred_element_type=f32)
        slot = jnp.where(hit, t * CAP + rank.astype(jnp.int32), slot)
    slot_ref[...] = slot
    local = (rm - r * ROWS_DEV + 1).astype(f32)
    small_sub = lax.broadcasted_iota(jnp.int32, (LANES, SRC), 0)
    small_lane = lax.broadcasted_iota(jnp.int32, (LANES, SRC), 1)
    packed = jnp.zeros((rows, SRC), f32)
    for k in range(CAP):
        value = jnp.where(slot == r * CAP + k, local, 0.0)
        to = (jnp.right_shift(small_sub, 5) * CAP + k == small_lane).astype(f32)
        packed = packed + jnp.dot(value, to, precision=highest, preferred_element_type=f32)
    slots = NR * NC * CAP
    wide_sub = lax.broadcasted_iota(jnp.int32, (SRC, slots), 0)
    wide_lane = lax.broadcasted_iota(jnp.int32, (SRC, slots), 1)
    repeat = (jnp.bitwise_and(wide_lane, SRC - 1) == wide_sub).astype(f32)
    spread = jnp.dot(packed, repeat, precision=highest, preferred_element_type=f32)
    flat = jnp.where(jnp.right_shift(wide_lane, 5) == wide_sub, spread, 0.0)
    flat = jnp.sum(flat, axis=0, keepdims=True)
    front_ref[...] = jnp.broadcast_to(flat.astype(jnp.int32) - 1, (SUB, slots))
    fetch = pltpu.make_async_copy(qv_ref, q_ref, sem)
    fetch.start()

    first_row = lax.rem((r * NC + c) * SRC, NR * NC * SRC // 2)
    for t in range(PANEL // TILE):
        at = slice(t * TILE, (t + 1) * TILE)
        ids = lax.broadcasted_iota(jnp.int32, (SRC, TILE), 0)
        pan_ref[:, at] = jnp.where(ids + first_row < stair_ref[child, t], ch_ref[:, at], 0.0)
    fetch.wait()
    sub_ids = lax.broadcasted_iota(jnp.int32, (SUB, LANES), 0) + first_row
    halves = QCOLS // LANES

    def one(m, carry):
        j = m // (NC // 2)
        n = lax.rem(m, NC // 2)
        found = []
        for cc in range(2):
            for h in range(halves):
                b = (n * 2 + cc) * (BLOCK_COLS // LANES) + j * halves + h
                q = q_ref[0, b]
                start = pl.multiple_of(q * LANES, LANES)
                after = pl.multiple_of(start + LANES, LANES)
                code = jnp.broadcast_to(code_ref[pl.ds(b, 1), :], (SUB, LANES))
                lane = jnp.bitwise_and(code, LANES - 1)
                limit = jnp.where(
                    code < LANES,
                    stair_ref[child, q // (TILE // LANES)],
                    stair_ref[child, (q + 1) // (TILE // LANES)],
                )
                limit = jnp.where(code < 0, 0, limit)
                for g in range(SRC // SUB):
                    v0 = ch_ref[g * SUB : (g + 1) * SUB, pl.ds(start, LANES)]
                    v1 = ch_ref[g * SUB : (g + 1) * SUB, pl.ds(after, LANES)]
                    g0 = jnp.take_along_axis(v0, lane, axis=1)
                    g1 = jnp.take_along_axis(v1, lane, axis=1)
                    v = jnp.where(code < LANES, g0, g1)
                    found.append((cc, h, g, jnp.where(sub_ids + g * SUB < limit, v, 0.0)))
        for cc, h, g, v in found:
            x_ref[j, n * 2 + cc, g * SUB : (g + 1) * SUB, h * LANES : (h + 1) * LANES] = v
        return carry

    lax.fori_loop(0, QUARTERS * NC // 2, one, 0)


def place_columns(children, row_map, column_map, staircase):
    vmem = pl.BlockSpec(memory_space=pltpu.VMEM)
    rows = row_map.shape[0] // LANES
    return pl.pallas_call(
        table_kernel,
        in_specs=[pl.BlockSpec(memory_space=pltpu.SMEM)] + [vmem] * 3,
        out_specs=[vmem] * 4,
        out_shape=[
            jax.ShapeDtypeStruct((QUARTERS, NC, SRC, QCOLS), f32),
            jax.ShapeDtypeStruct((SRC, PANEL), f32),
            jax.ShapeDtypeStruct((rows, LANES), jnp.int32),
            jax.ShapeDtypeStruct((SUB, NR * NC * CAP), jnp.int32),
        ],
        scratch_shapes=[
            pltpu.VMEM((FRONT_BLOCKS, LANES), jnp.int32),
            pltpu.VMEM((SUB, FRONT_BLOCKS), jnp.int32),
            pltpu.SMEM((SUB, FRONT_BLOCKS), jnp.int32),
            pltpu.SemaphoreType.DMA,
        ],
        cost_estimate=pl.CostEstimate(flops=400_000_000, bytes_accessed=4_000_000, transcendentals=0),
    )(staircase, row_map.reshape(rows, LANES), column_map, children)


def across_lanes(v, lane):
    return jnp.broadcast_to(v[:, lane : lane + 1], (SUB, LANES))

def across_rows(v, row):
    return jnp.broadcast_to(v[row : row + 1, :], (SUB, LANES))

def inverse_of_block(block, unit, write):
    groups = LANES // SUB
    sub = lax.broadcasted_iota(jnp.int32, (SUB, LANES), 0)
    for g in range(groups):
        cols = [across_lanes(block[g], SUB * g + m) for m in range(SUB)]
        a = {(i, m): across_rows(cols[m], i) for m in range(SUB) for i in range(m, SUB)}
        low = {}
        inv = {}
        for k in range(SUB):
            inv[k, k] = lax.rsqrt(a[k, k])
            for i in range(k + 1, SUB):
                low[i, k] = a[i, k] * inv[k, k]
            for i in range(k + 1, SUB):
                for m in range(k + 1, i + 1):
                    a[i, m] = a[i, m] - low[i, k] * low[m, k]
        for i in range(1, SUB):
            for k in range(i):
                acc = low[i, k] * inv[k, k]
                for m in range(k + 1, i):
                    acc = acc + low[i, m] * inv[m, k]
                inv[i, k] = -inv[i, i] * acc
        zero = jnp.zeros((SUB, LANES), f32)
        down = []
        for k in range(SUB):
            col = zero
            for i in range(k, SUB):
                col = jnp.where(sub == i, inv[i, k], col)
            down.append(col)
        up = []
        for k in range(SUB):
            col = zero
            for i in range(k + 1):
                col = jnp.where(sub == i, inv[k, i], col)
            up.append(col)

        def apply(cols, v):
            terms = [cols[k] * across_rows(v, k) for k in range(SUB)]
            while len(terms) > 1:
                terms = [terms[i] + terms[i + 1] for i in range(0, len(terms), 2)]
            return terms[0]

        done = apply(down, unit[g])
        write(g, done)
        if g + 1 < groups:
            z = apply(up, apply(down, block[g]))
            zu = apply(up, done)
            zr = [across_rows(z, m) for m in range(SUB)]
            zur = [across_rows(zu, m) for m in range(SUB)]
            for i in range(g + 1, groups):
                mult = [across_lanes(block[i], SUB * g + m) for m in range(SUB)]
                t = [mult[m] * zr[m] for m in range(SUB)]
                u = [mult[m] * zur[m] for m in range(SUB)]
                while len(t) > 1:
                    t = [t[j] + t[j + 1] for j in range(0, len(t), 2)]
                    u = [u[j] + u[j + 1] for j in range(0, len(u), 2)]
                block[i] = block[i] - t[0]
                unit[i] = unit[i] - u[0]


def three_parts(x):
    hi = x.astype(bf16)
    rest = x - hi.astype(f32)
    mid = rest.astype(bf16)
    low = (rest - mid.astype(f32)).astype(bf16)
    return jnp.concatenate([hi, mid, low], axis=0)


def two_parts(x):
    hi = x.astype(bf16)
    return hi, (x - hi.astype(f32)).astype(bf16)


class GatherCt:
    def __init__(self, source, dest, r, c, s1, r1, s2, r2):
        self.source, self.dest, self.r, self.c = source, dest, r, c
        self.sems = (s1, r1, s2, r2)
        self.first, self.second = [], []

    def along(self, half, d):
        z, y = self.c // SIDE, lax.rem(self.c, SIDE)
        if half == 0:
            return z * SIDE + lax.rem(y + d, SIDE)
        return lax.rem(z + d, SIDE) * SIDE + y

    def send(self, src, half, owner, to, ss, rs):
        copy = pltpu.make_async_remote_copy(
            src_ref=src,
            dst_ref=self.dest(half, owner),
            send_sem=ss,
            recv_sem=rs,
            device_id=(self.r, to),
            device_id_type=MESH,
        )
        copy.start()
        return copy

    def start(self):
        s1, r1, s2, r2 = self.sems
        for d in range(1, SIDE):
            for h in range(2):
                to = self.along(h, d)
                copy = self.send(self.source(h), h, self.c, to, s1.at[h, d - 1], r1.at[h, d - 1])
                self.first.append(copy)
        for d in range(1, SIDE):
            for h in range(2):
                to = self.along(1 - h, d)
                copy = self.send(
                    self.source(h), h, self.c, to, s2.at[h, 0, d - 1], r2.at[h, 0, d - 1]
                )
                self.second.append(copy)

    def forward(self):
        s1, r1, s2, r2 = self.sems
        position = 0
        for p in range(1, SIDE):
            for h in range(2):
                self.first[position].wait()
                position += 1
                owner = self.along(h, SIDE - p)
                for d in range(1, SIDE):
                    to = self.along(1 - h, d)
                    copy = self.send(
                        self.dest(h, owner), h, owner, to, s2.at[h, p, d - 1], r2.at[h, p, d - 1]
                    )
                    self.second.append(copy)

    def finish(self):
        for copy in self.second:
            copy.wait()


def front_kernel(
    x_ref, pan_ref, slot_ref, order_ref,
    front_ref, rows_ref, sum_ref, inv_ref,
    sel_ref, fs_ref, as_ref, perm, parts, po, chunk, ap, apt, gpart, gin, gsum, gbuf, fp, routed, work, small,
    part, ain, half, bin_ref, mine, full,
    p1s, p1r, a1s, a1r, a2s, a2r, c1s, c1r, c2s, c2r, g1s, g1r, g2s, g2r, p3s, p3r,
    t1s, t1r, t2s, t2r, sa, ra, sb, rb, sc, rc, sd, rd,
):
    r = lax.axis_index("rt")
    c = lax.axis_index("ct")
    core = lax.rem(r, 2)
    x = r // 2
    sibling = r + 1 - 2 * core
    chip_peers = [2 * lax.rem(x + d, CHIPS) + core for d in range(1, CHIPS)]
    barrier = pltpu.get_barrier_semaphore()
    for d in range(1, NR):
        pl.semaphore_signal(barrier, inc=1, device_id=(lax.rem(r + d, NR), c), device_id_type=MESH)
    for e in range(1, NC):
        pl.semaphore_signal(barrier, inc=1, device_id=(r, lax.rem(c + e, NC)), device_id_type=MESH)

    pl.semaphore_wait(barrier, NR + NC - 2)

    def send(src, dst, ss, rs, rt, ct):
        copy = pltpu.make_async_remote_copy(
            src_ref=src, dst_ref=dst, send_sem=ss, recv_sem=rs, device_id=(rt, ct), device_id_type=MESH
        )
        copy.start()
        return copy

    def to_rt(src_of, dst, ss, rs):
        copies = []
        for d in range(1, NR):
            t = lax.rem(r + d, NR)
            copies.append(send(src_of(t), dst, ss.at[d - 1], rs.at[d - 1], t, c))
        return copies

    def wait_all(copies):
        for copy in copies:
            copy.wait()

    def selections():
        lane = lax.broadcasted_iota(jnp.int32, (NR * CAP, LANES), 1)
        ids = lax.broadcasted_iota(jnp.int32, (NR * CAP, LANES), 0)
        per = LANES // SRC
        for u in range(NC // per):
            row = jnp.broadcast_to(slot_ref[pl.ds(r * (NC // per) + u, 1), :], (NR * CAP, LANES))
            for v in range(per):
                turned = [
                    pltpu.roll(row, (g - v) % per * SRC, 1) if g != v else row for g in range(3)
                ]
                slots = jnp.where(lane < SRC, turned[0], jnp.where(lane < 2 * SRC, turned[1], turned[2]))
                chosen = (slots == ids).astype(f32).astype(bf16)
                sel_ref[u * per + v] = chosen[:, : 3 * SRC]

    def start_columns(j):
        copies = []
        for e in range(1, NC):
            to = lax.rem(c + e, NC)
            copies.append(
                send(x_ref.at[j, to], fp.at[j, c], t1s.at[j, e - 1], t1r.at[j, e - 1], r, to)
            )
        fp[j, c] = x_ref[j, c]
        return copies

    def route(j, copies):
        wait_all(copies)

        def four(n, carry):
            done = []
            for i in range(4):
                s = n * 4 + i
                y = jnp.dot(sel_ref[s], three_parts(fp[j, s]), preferred_element_type=f32)
                done.append((s, y))
            for s, y in done:
                at = pl.ds(pl.multiple_of(s * CAP, CAP), CAP)
                routed[j, :, at, :] = y.reshape(NR, CAP, QCOLS)
            return carry

        lax.fori_loop(0, NC // 4, four, 0)
        sends = to_rt(lambda t: routed.at[j, t], fs_ref.at[j, r], t2s.at[j], t2r.at[j])
        fs_ref[j, r] = routed[j, r]
        return sends

    def order(load, store, width):
        def split(n, carry):
            at = pl.ds(pl.multiple_of(n * LANES, LANES), LANES)
            rest = load(n)
            for p in range(3):
                piece = rest.astype(bf16)
                parts[p, at, :width] = piece
                rest = rest - piece.astype(f32)
            return carry

        lax.fori_loop(0, NR, split, 0)

        def rows_of(n, carry):
            at = pl.ds(pl.multiple_of(n * LANES, LANES), LANES)
            y = jnp.dot(perm[at, :], parts[0, :, :width], preferred_element_type=f32)
            y = y + jnp.dot(perm[at, :], parts[1, :, :width], preferred_element_type=f32)
            y = y + jnp.dot(perm[at, :], parts[2, :, :width], preferred_element_type=f32)
            store(at, y)
            return carry

        lax.fori_loop(0, ROWS_DEV // LANES, rows_of, 0)

    def order_columns(j, copies):
        wait_all(copies)

        def store(at, y):
            front_ref[at, j * QCOLS : (j + 1) * QCOLS] = y

        order(lambda n: fs_ref[j, n], store, QCOLS)

    def make_perm():
        def one(n, carry):
            at = pl.ds(pl.multiple_of(n * LANES, LANES), LANES)
            shape = (LANES, NR * NC * CAP)
            ids = lax.broadcasted_iota(jnp.int32, shape, 0) + n * LANES
            perm[at, :] = (jnp.broadcast_to(order_ref[0:1, :], shape) == ids).astype(f32).astype(bf16)
            return carry

        lax.fori_loop(0, ROWS_DEV // LANES, one, 0)

    panel = GatherCt(
        lambda h: pan_ref.at[pl.ds(h * SRC // 2, SRC // 2)],
        lambda h, o: ap.at[o, pl.ds(h * SRC // 2, SRC // 2)],
        r, c, a1s, a1r, a2s, a2r,
    )
    rows = GatherCt(
        lambda h: chunk.at[pl.ds(h * NR // 2, NR // 2)],
        lambda h, o: as_ref.at[pl.ds(h * NR // 2, NR // 2), o],
        r, c, c1s, c1r, c2s, c2r,
    )
    grams = GatherCt(
        lambda h: gsum.at[pl.ds(h * len(PAIRS) // 2, len(PAIRS) // 2)],
        lambda h, o: gbuf.at[o, pl.ds(h * len(PAIRS) // 2, len(PAIRS) // 2)],
        r, c, g1s, g1r, g2s, g2r,
    )

    panel.start()
    ap[c] = pan_ref[...]
    columns = [start_columns(0)]
    panel.forward()
    selections()
    columns.append(start_columns(1))
    panel.finish()
    columns.append(start_columns(2))
    columns.append(start_columns(3))
    po[...] = jnp.dot(
        sel_ref[c], three_parts(pan_ref[...]), preferred_element_type=f32
    ).reshape(NR, CAP, PANEL)
    whole = ap[...].reshape(NC * SRC, PANEL)
    apt[...] = whole.T
    for i in range(PANEL // LANES):
        block = jnp.dot(
            apt[i * LANES : (i + 1) * LANES, :],
            ap[:, :, i * LANES :].reshape(NC * SRC, PANEL - i * LANES),
            precision=highest,
            preferred_element_type=f32,
        )
        for j in range(i, PANEL // LANES):
            piece = block[:, (j - i) * LANES : (j - i + 1) * LANES]
            gpart[:, PAIRS.index((i, j))] = piece.reshape(NC, SUB, LANES)
    gram_sends = to_rt(lambda t: gpart.at[c], gin.at[r], p3s, p3r)
    gin[r] = gpart[c]
    chunks = to_rt(lambda t: po.at[t], chunk.at[r], p1s, p1r)
    chunk[r] = po[r]

    routes = [route(0, columns[0])]
    wait_all(gram_sends)
    total = gin[0]
    for t in range(1, NR):
        total = total + gin[t]
    gsum[...] = total
    grams.start()
    gbuf[c] = total
    routes.append(route(1, columns[1]))
    grams.forward()
    wait_all(chunks)
    rows.start()
    as_ref[:, c] = chunk[...]
    routes.append(route(2, columns[2]))
    grams.finish()
    for n, (i, j) in enumerate(PAIRS):
        work[i * LANES : (i + 1) * LANES, j * LANES : (j + 1) * LANES] = gbuf[:, n].reshape(LANES, LANES)
    ids = lax.broadcasted_iota(jnp.int32, (PANEL, PANEL), 0)
    lanes = lax.broadcasted_iota(jnp.int32, (PANEL, PANEL), 1)
    work[:, PANEL:] = jnp.where(ids == lanes, 1.0, 0.0).astype(f32)
    routes.append(route(3, columns[3]))
    rows.forward()

    def product(n, carry):
        i = n // QUARTERS
        j = lax.rem(n, QUARTERS)
        ah, al = two_parts(apt[pl.ds(pl.multiple_of(i * LANES, LANES), LANES), :])
        bh, bl = two_parts(fp[j].reshape(NC * SRC, QCOLS))
        y = jnp.dot(ah, bh, preferred_element_type=f32)
        y = y + jnp.dot(ah, bl, preferred_element_type=f32)
        y = y + jnp.dot(al, bh, preferred_element_type=f32)
        y = y.reshape(LANES // SLICE, SLICE, QCOLS)
        at = pl.ds(lax.rem(i, 2) * (LANES // SLICE), LANES // SLICE)
        part[i // 2, at, :, pl.ds(pl.multiple_of(j * QCOLS, QCOLS), QCOLS)] = y
        return carry

    lax.fori_loop(0, QUARTERS * (PANEL // LANES), product, 0)
    swap = send(part.at[1 - core], ain, sa, ra, sibling, c)

    factor_step(0, work, small)
    swap.wait()
    half[...] = part[core] + ain[...]
    spread = [
        send(half.at[peer // 2], bin_ref.at[d], sb.at[d], rb.at[d], peer, c)
        for d, peer in enumerate(chip_peers)
    ]
    make_perm()
    factor_step(1, work, small)
    order_columns(0, routes[0])
    wait_all(spread)
    mine[...] = (half[x] + bin_ref[0]) + (bin_ref[1] + bin_ref[2])
    spread = [
        send(mine, full.at[core, x], sc.at[d], rc.at[d], peer, c) for d, peer in enumerate(chip_peers)
    ]
    last = [send(mine, full.at[core, x], sd.at[CHIPS - 1], rd.at[CHIPS - 1], sibling, c)]
    full[core, x] = mine[...]
    factor_step(2, work, small)
    factor_step(3, work, small)
    inv_ref[...] = work[:, PANEL:]
    for d, copy in enumerate(spread):
        copy.wait()
        owner = lax.rem(x + CHIPS - d - 1, CHIPS)
        last.append(
            send(full.at[core, owner], full.at[core, owner], sd.at[d], rd.at[d], sibling, c)
        )
    rows.finish()

    def store_rows(lane_at):
        def store(at, y):
            rows_ref[at, lane_at : lane_at + QCOLS] = y

        return store

    for n in range(PANEL // QCOLS):
        at = slice(n * QCOLS, (n + 1) * QCOLS)
        order(lambda t: as_ref[t].reshape(NC * CAP, PANEL)[:, at], store_rows(n * QCOLS), QCOLS)
    for j in range(1, QUARTERS):
        order_columns(j, routes[j])
    wait_all(last)
    sum_ref[...] = full[...].reshape(PANEL, BLOCK_COLS)


def factor_step(b, work, small):
    o = b * LANES
    lane = lax.broadcasted_iota(jnp.int32, (SUB, LANES), 1)
    sub = lax.broadcasted_iota(jnp.int32, (SUB, LANES), 0)
    block = [work[o + SUB * g : o + SUB * (g + 1), o : o + LANES] for g in range(LANES // SUB)]
    unit = [jnp.where(lane == sub + SUB * g, 1.0, 0.0).astype(f32) for g in range(LANES // SUB)]

    def write(g, v):
        small[SUB * g : SUB * (g + 1), :] = v

    inverse_of_block(block, unit, write)
    end = PANEL + o + LANES
    row = jnp.dot(
        small[...], work[o : o + LANES, o:end], precision=highest, preferred_element_type=f32
    )
    work[o : o + LANES, o:end] = row
    for p in range(o + LANES, PANEL, LANES):
        mult = row[:, p - o : p - o + LANES]
        work[p : p + LANES, p:end] = work[p : p + LANES, p:end] - jnp.dot(
            mult.T, row[:, p - o :], precision=highest, preferred_element_type=f32
        )


def build_front(columns, panel, slot, order):
    slots = NC * CAP
    vmem = pltpu.VMEM
    dma = pltpu.SemaphoreType.DMA
    n = len(PAIRS)
    ring = [dma((2, SIDE - 1)), dma((2, SIDE - 1)), dma((2, SIDE, SIDE - 1)), dma((2, SIDE, SIDE - 1))]
    return pl.pallas_call(
        front_kernel,
        in_specs=[pl.BlockSpec(memory_space=pltpu.VMEM)] * 4,
        out_specs=[pl.BlockSpec(memory_space=pltpu.VMEM)] * 4,
        out_shape=[
            jax.ShapeDtypeStruct((ROWS_DEV, BLOCK_COLS), f32),
            jax.ShapeDtypeStruct((ROWS_DEV, PANEL), f32),
            jax.ShapeDtypeStruct((PANEL, BLOCK_COLS), f32),
            jax.ShapeDtypeStruct((PANEL, PANEL), f32),
        ],
        scratch_shapes=[
            vmem((NC, NR * CAP, 3 * SRC), bf16),
            vmem((QUARTERS, NR, slots, QCOLS), f32),
            vmem((NR, NC, CAP, PANEL), f32),
            vmem((ROWS_DEV, NR * slots), bf16),
            vmem((3, NR * slots, QCOLS), bf16),
            vmem((NR, CAP, PANEL), f32),
            vmem((NR, CAP, PANEL), f32),
            vmem((NC, SRC, PANEL), f32),
            vmem((PANEL, NC * SRC), f32),
            vmem((NC, n, SUB, LANES), f32),
            vmem((NR, n, SUB, LANES), f32),
            vmem((n, SUB, LANES), f32),
            vmem((NC, n, SUB, LANES), f32),
            vmem((QUARTERS, NC, SRC, QCOLS), f32),
            vmem((QUARTERS, NR, slots, QCOLS), f32),
            vmem((PANEL, 2 * PANEL), f32),
            vmem((LANES, LANES), f32),
            vmem((2, CHIPS, SLICE, BLOCK_COLS), f32),
            vmem((CHIPS, SLICE, BLOCK_COLS), f32),
            vmem((CHIPS, SLICE, BLOCK_COLS), f32),
            vmem((CHIPS - 1, SLICE, BLOCK_COLS), f32),
            vmem((SLICE, BLOCK_COLS), f32),
            vmem((2, CHIPS, SLICE, BLOCK_COLS), f32),
            dma((NR - 1,)),
            dma((NR - 1,)),
            *ring,
            *ring,
            *ring,
            dma((NR - 1,)),
            dma((NR - 1,)),
            dma((QUARTERS, NC - 1)),
            dma((QUARTERS, NC - 1)),
            dma((QUARTERS, NR - 1)),
            dma((QUARTERS, NR - 1)),
            dma(()),
            dma(()),
            dma((CHIPS - 1,)),
            dma((CHIPS - 1,)),
            dma((CHIPS - 1,)),
            dma((CHIPS - 1,)),
            dma((CHIPS,)),
            dma((CHIPS,)),
        ],
        compiler_params=pltpu.CompilerParams(collective_id=0, has_side_effects=True),
        cost_estimate=pl.CostEstimate(
            flops=3_000_000_000, bytes_accessed=300_000_000, transcendentals=0
        ),
    )(columns, panel, slot, order)


def shards(children, row_map, column_map, staircase):
    placed = place_columns(children, row_map, column_map, staircase)
    front_block, panel_block, projected, inverse = build_front(*placed)
    basis = lax.dot_general(
        inverse, panel_block, (((1,), (1,)), ((), ())), precision=high, preferred_element_type=f32
    )
    factor_rows = jnp.dot(inverse, projected, precision=high, preferred_element_type=f32)
    update = lax.dot_general(
        basis, factor_rows, (((0,), (0,)), ((), ())), precision=high, preferred_element_type=f32
    )
    return (factor_rows, basis, front_block - update)


def solution(mesh):
    placed = (P(("rt", "ct"), None), P(), P(), P())
    return jax.shard_map(
        shards,
        mesh=mesh,
        in_specs=placed,
        out_specs=(P(None, "ct"), P(None, "rt"), P("rt", "ct")),
        check_vma=False,
    )
```

```python
import functools

import jax
import jax.numpy as jnp
from jax import lax
from jax.experimental import pallas as pl
from jax.experimental.pallas import tpu as pltpu
from jax.sharding import PartitionSpec as P

TILE = 256
PANEL = 512
SUB = 8
LANES = 128
NR = 8
NC = 16
SRC = 32
CAP = 8
ROWS_DEV = 512
BLOCK_COLS = 1024
FRONT_COLS = NC * BLOCK_COLS
FRONT_BLOCKS = FRONT_COLS // LANES
QUARTERS = 4
QCOLS = BLOCK_COLS // QUARTERS
SIDE = 4
CHIPS = NR // 2
SLICE = PANEL // NR
PAIRS = [(i, j) for i in range(PANEL // LANES) for j in range(i, PANEL // LANES)]

highest = lax.Precision.HIGHEST
high = lax.Precision.HIGH
f32 = jnp.float32
bf16 = jnp.bfloat16
MESH = pl.DeviceIdType.MESH


def table_kernel(
    stair_ref, row_ref, col_ref, ch_ref, x_ref, pan_ref, slot_ref, front_ref, code_ref, qv_ref, q_ref, sem
):
    r = lax.axis_index("rt")
    c = lax.axis_index("ct")
    child = r // (NR // 2)
    child_cols = col_ref.shape[1]
    rows = row_ref.shape[0]
    sub = lax.broadcasted_iota(jnp.int32, (LANES, LANES), 0)
    lane = lax.broadcasted_iota(jnp.int32, (LANES, LANES), 1)

    step = child_cols // 6
    ids = lax.broadcasted_iota(jnp.int32, (LANES, step), 0)
    present = jnp.zeros((LANES, LANES), f32)
    for n in range(6):
        cm = col_ref[pl.ds(child, 1), n * step : (n + 1) * step]
        cm = jnp.broadcast_to(cm, (LANES, step))
        upper = (jnp.right_shift(cm, 7) == ids).astype(f32).astype(bf16)
        lower = (jnp.bitwise_and(cm, LANES - 1) == ids).astype(f32).astype(bf16)
        present = present + lax.dot_general(
            upper, lower, (((1,), (1,)), ((), ())), preferred_element_type=f32
        )
    flags = present.astype(bf16)
    before = (sub < lane).astype(f32).astype(bf16)
    inside = jnp.dot(flags, before, preferred_element_type=f32)
    above = jnp.dot((lane < sub).astype(f32).astype(bf16), flags, preferred_element_type=f32)
    starts = jnp.sum(above, axis=1, keepdims=True).astype(jnp.int32)
    last = child_cols // LANES - 2
    q = jnp.minimum(jnp.right_shift(starts, 7), last)
    code = starts - q * LANES + inside.astype(jnp.int32)
    code_ref[...] = jnp.where(present > 0.5, code, -1)
    across = lax.dot_general(
        jnp.ones((SUB, LANES), bf16), above.astype(bf16), (((1,), (1,)), ((), ())),
        preferred_element_type=f32,
    )
    qv_ref[...] = jnp.minimum(jnp.right_shift(across.astype(jnp.int32), 7), last)

    rm = row_ref[...]
    tile = jnp.right_shift(rm, 9)
    group = jnp.right_shift(sub, 5) == jnp.right_shift(lane, 5)
    earlier = (group & (sub < lane)).astype(f32).astype(bf16)
    slot = jnp.zeros((rows, LANES), jnp.int32)
    for t in range(NR):
        hit = tile == t
        rank = jnp.dot(hit.astype(f32).astype(bf16), earlier, preferred_element_type=f32)
        slot = jnp.where(hit, t * CAP + rank.astype(jnp.int32), slot)
    slot_ref[...] = slot
    local = (rm - r * ROWS_DEV + 1).astype(f32)
    small_sub = lax.broadcasted_iota(jnp.int32, (LANES, SRC), 0)
    small_lane = lax.broadcasted_iota(jnp.int32, (LANES, SRC), 1)
    packed = jnp.zeros((rows, SRC), f32)
    for k in range(CAP):
        value = jnp.where(slot == r * CAP + k, local, 0.0)
        to = (jnp.right_shift(small_sub, 5) * CAP + k == small_lane).astype(f32)
        packed = packed + jnp.dot(value, to, precision=highest, preferred_element_type=f32)
    slots = NR * NC * CAP
    wide_sub = lax.broadcasted_iota(jnp.int32, (SRC, slots), 0)
    wide_lane = lax.broadcasted_iota(jnp.int32, (SRC, slots), 1)
    repeat = (jnp.bitwise_and(wide_lane, SRC - 1) == wide_sub).astype(f32)
    spread = jnp.dot(packed, repeat, precision=highest, preferred_element_type=f32)
    flat = jnp.where(jnp.right_shift(wide_lane, 5) == wide_sub, spread, 0.0)
    flat = jnp.sum(flat, axis=0, keepdims=True)
    front_ref[...] = jnp.broadcast_to(flat.astype(jnp.int32) - 1, (SUB, slots))
    fetch = pltpu.make_async_copy(qv_ref, q_ref, sem)
    fetch.start()

    first_row = lax.rem((r * NC + c) * SRC, NR * NC * SRC // 2)
    for t in range(PANEL // TILE):
        at = slice(t * TILE, (t + 1) * TILE)
        ids = lax.broadcasted_iota(jnp.int32, (SRC, TILE), 0)
        pan_ref[:, at] = jnp.where(ids + first_row < stair_ref[child, t], ch_ref[:, at], 0.0)
    fetch.wait()
    sub_ids = lax.broadcasted_iota(jnp.int32, (SUB, LANES), 0) + first_row
    halves = QCOLS // LANES

    def one(m, carry):
        j = m // (NC // 2)
        n = lax.rem(m, NC // 2)
        found = []
        for cc in range(2):
            for h in range(halves):
                b = (n * 2 + cc) * (BLOCK_COLS // LANES) + j * halves + h
                q = q_ref[0, b]
                start = pl.multiple_of(q * LANES, LANES)
                after = pl.multiple_of(start + LANES, LANES)
                code = jnp.broadcast_to(code_ref[pl.ds(b, 1), :], (SUB, LANES))
                lane = jnp.bitwise_and(code, LANES - 1)
                limit = jnp.where(
                    code < LANES,
                    stair_ref[child, q // (TILE // LANES)],
                    stair_ref[child, (q + 1) // (TILE // LANES)],
                )
                limit = jnp.where(code < 0, 0, limit)
                for g in range(SRC // SUB):
                    v0 = ch_ref[g * SUB : (g + 1) * SUB, pl.ds(start, LANES)]
                    v1 = ch_ref[g * SUB : (g + 1) * SUB, pl.ds(after, LANES)]
                    g0 = jnp.take_along_axis(v0, lane, axis=1)
                    g1 = jnp.take_along_axis(v1, lane, axis=1)
                    v = jnp.where(code < LANES, g0, g1)
                    found.append((cc, h, g, jnp.where(sub_ids + g * SUB < limit, v, 0.0)))
        for cc, h, g, v in found:
            x_ref[j, n * 2 + cc, g * SUB : (g + 1) * SUB, h * LANES : (h + 1) * LANES] = v
        return carry

    lax.fori_loop(0, QUARTERS * NC // 2, one, 0)


def place_columns(children, row_map, column_map, staircase):
    vmem = pl.BlockSpec(memory_space=pltpu.VMEM)
    rows = row_map.shape[0] // LANES
    return pl.pallas_call(
        table_kernel,
        in_specs=[pl.BlockSpec(memory_space=pltpu.SMEM)] + [vmem] * 3,
        out_specs=[vmem] * 4,
        out_shape=[
            jax.ShapeDtypeStruct((QUARTERS, NC, SRC, QCOLS), f32),
            jax.ShapeDtypeStruct((SRC, PANEL), f32),
            jax.ShapeDtypeStruct((rows, LANES), jnp.int32),
            jax.ShapeDtypeStruct((SUB, NR * NC * CAP), jnp.int32),
        ],
        scratch_shapes=[
            pltpu.VMEM((FRONT_BLOCKS, LANES), jnp.int32),
            pltpu.VMEM((SUB, FRONT_BLOCKS), jnp.int32),
            pltpu.SMEM((SUB, FRONT_BLOCKS), jnp.int32),
            pltpu.SemaphoreType.DMA,
        ],
        cost_estimate=pl.CostEstimate(flops=400_000_000, bytes_accessed=4_000_000, transcendentals=0),
    )(staircase, row_map.reshape(rows, LANES), column_map, children)


def across_lanes(v, lane):
    return jnp.broadcast_to(v[:, lane : lane + 1], (SUB, LANES))

def across_rows(v, row):
    return jnp.broadcast_to(v[row : row + 1, :], (SUB, LANES))

def inverse_of_block(block, unit, write):
    groups = LANES // SUB
    sub = lax.broadcasted_iota(jnp.int32, (SUB, LANES), 0)
    for g in range(groups):
        cols = [across_lanes(block[g], SUB * g + m) for m in range(SUB)]
        a = {(i, m): across_rows(cols[m], i) for m in range(SUB) for i in range(m, SUB)}
        low = {}
        inv = {}
        for k in range(SUB):
            inv[k, k] = lax.rsqrt(a[k, k])
            for i in range(k + 1, SUB):
                low[i, k] = a[i, k] * inv[k, k]
            for i in range(k + 1, SUB):
                for m in range(k + 1, i + 1):
                    a[i, m] = a[i, m] - low[i, k] * low[m, k]
        for i in range(1, SUB):
            for k in range(i):
                acc = low[i, k] * inv[k, k]
                for m in range(k + 1, i):
                    acc = acc + low[i, m] * inv[m, k]
                inv[i, k] = -inv[i, i] * acc
        zero = jnp.zeros((SUB, LANES), f32)
        down = []
        for k in range(SUB):
            col = zero
            for i in range(k, SUB):
                col = jnp.where(sub == i, inv[i, k], col)
            down.append(col)
        up = []
        for k in range(SUB):
            col = zero
            for i in range(k + 1):
                col = jnp.where(sub == i, inv[k, i], col)
            up.append(col)

        def apply(cols, v):
            terms = [cols[k] * across_rows(v, k) for k in range(SUB)]
            while len(terms) > 1:
                terms = [terms[i] + terms[i + 1] for i in range(0, len(terms), 2)]
            return terms[0]

        done = apply(down, unit[g])
        write(g, done)
        if g + 1 < groups:
            z = apply(up, apply(down, block[g]))
            zu = apply(up, done)
            zr = [across_rows(z, m) for m in range(SUB)]
            zur = [across_rows(zu, m) for m in range(SUB)]
            for i in range(g + 1, groups):
                mult = [across_lanes(block[i], SUB * g + m) for m in range(SUB)]
                t = [mult[m] * zr[m] for m in range(SUB)]
                u = [mult[m] * zur[m] for m in range(SUB)]
                while len(t) > 1:
                    t = [t[j] + t[j + 1] for j in range(0, len(t), 2)]
                    u = [u[j] + u[j + 1] for j in range(0, len(u), 2)]
                block[i] = block[i] - t[0]
                unit[i] = unit[i] - u[0]


def three_parts(x):
    hi = x.astype(bf16)
    rest = x - hi.astype(f32)
    mid = rest.astype(bf16)
    low = (rest - mid.astype(f32)).astype(bf16)
    return jnp.concatenate([hi, mid, low], axis=0)


def two_parts(x):
    hi = x.astype(bf16)
    return hi, (x - hi.astype(f32)).astype(bf16)


class GatherCt:
    def __init__(self, source, dest, r, c, s1, r1, s2, r2):
        self.source, self.dest, self.r, self.c = source, dest, r, c
        self.sems = (s1, r1, s2, r2)
        self.first, self.second = [], []

    def along(self, half, d):
        z, y = self.c // SIDE, lax.rem(self.c, SIDE)
        if half == 0:
            return z * SIDE + lax.rem(y + d, SIDE)
        return lax.rem(z + d, SIDE) * SIDE + y

    def send(self, src, half, owner, to, ss, rs):
        copy = pltpu.make_async_remote_copy(
            src_ref=src,
            dst_ref=self.dest(half, owner),
            send_sem=ss,
            recv_sem=rs,
            device_id=(self.r, to),
            device_id_type=MESH,
        )
        copy.start()
        return copy

    def start(self):
        s1, r1, s2, r2 = self.sems
        for d in range(1, SIDE):
            for h in range(2):
                to = self.along(h, d)
                copy = self.send(self.source(h), h, self.c, to, s1.at[h, d - 1], r1.at[h, d - 1])
                self.first.append(copy)
        for d in range(1, SIDE):
            for h in range(2):
                to = self.along(1 - h, d)
                copy = self.send(
                    self.source(h), h, self.c, to, s2.at[h, 0, d - 1], r2.at[h, 0, d - 1]
                )
                self.second.append(copy)

    def forward(self):
        s1, r1, s2, r2 = self.sems
        position = 0
        for p in range(1, SIDE):
            for h in range(2):
                self.first[position].wait()
                position += 1
                owner = self.along(h, SIDE - p)
                for d in range(1, SIDE):
                    to = self.along(1 - h, d)
                    copy = self.send(
                        self.dest(h, owner), h, owner, to, s2.at[h, p, d - 1], r2.at[h, p, d - 1]
                    )
                    self.second.append(copy)

    def finish(self):
        for copy in self.second:
            copy.wait()


def front_kernel(
    x_ref, pan_ref, slot_ref, order_ref,
    front_ref, rows_ref, sum_ref, inv_ref,
    sel_ref, fs_ref, as_ref, perm, parts, po, chunk, ap, apt, gpart, gin, gsum, gbuf, fp, routed, work, small,
    part, ain, half, bin_ref, mine, full,
    p1s, p1r, a1s, a1r, a2s, a2r, c1s, c1r, c2s, c2r, g1s, g1r, g2s, g2r, p3s, p3r,
    t1s, t1r, t2s, t2r, sa, ra, sb, rb, sc, rc, sd, rd,
):
    r = lax.axis_index("rt")
    c = lax.axis_index("ct")
    core = lax.rem(r, 2)
    x = r // 2
    sibling = r + 1 - 2 * core
    chip_peers = [2 * lax.rem(x + d, CHIPS) + core for d in range(1, CHIPS)]
    barrier = pltpu.get_barrier_semaphore()
    for d in range(1, NR):
        pl.semaphore_signal(barrier, inc=1, device_id=(lax.rem(r + d, NR), c), device_id_type=MESH)
    for e in range(1, NC):
        pl.semaphore_signal(barrier, inc=1, device_id=(r, lax.rem(c + e, NC)), device_id_type=MESH)

    pl.semaphore_wait(barrier, NR + NC - 2)

    def send(src, dst, ss, rs, rt, ct):
        copy = pltpu.make_async_remote_copy(
            src_ref=src, dst_ref=dst, send_sem=ss, recv_sem=rs, device_id=(rt, ct), device_id_type=MESH
        )
        copy.start()
        return copy

    def to_rt(src_of, dst, ss, rs):
        copies = []
        for d in range(1, NR):
            t = lax.rem(r + d, NR)
            copies.append(send(src_of(t), dst, ss.at[d - 1], rs.at[d - 1], t, c))
        return copies

    def wait_all(copies):
        for copy in copies:
            copy.wait()

    def selections():
        lane = lax.broadcasted_iota(jnp.int32, (NR * CAP, LANES), 1)
        ids = lax.broadcasted_iota(jnp.int32, (NR * CAP, LANES), 0)
        per = LANES // SRC
        for u in range(NC // per):
            row = jnp.broadcast_to(slot_ref[pl.ds(r * (NC // per) + u, 1), :], (NR * CAP, LANES))
            for v in range(per):
                turned = [
                    pltpu.roll(row, (g - v) % per * SRC, 1) if g != v else row for g in range(3)
                ]
                slots = jnp.where(lane < SRC, turned[0], jnp.where(lane < 2 * SRC, turned[1], turned[2]))
                chosen = (slots == ids).astype(f32).astype(bf16)
                sel_ref[u * per + v] = chosen[:, : 3 * SRC]

    def start_columns(j):
        copies = []
        for e in range(1, NC):
            to = lax.rem(c + e, NC)
            copies.append(
                send(x_ref.at[j, to], fp.at[j, c], t1s.at[j, e - 1], t1r.at[j, e - 1], r, to)
            )
        fp[j, c] = x_ref[j, c]
        return copies

    def select_rows(j, copies):
        wait_all(copies)

        def four(n, carry):
            done = []
            for i in range(4):
                s = n * 4 + i
                y = jnp.dot(sel_ref[s], three_parts(fp[j, s]), preferred_element_type=f32)
                done.append((s, y))
            for s, y in done:
                at = pl.ds(pl.multiple_of(s * CAP, CAP), CAP)
                routed[j, :, at, :] = y.reshape(NR, CAP, QCOLS)
            return carry

        lax.fori_loop(0, NC // 4, four, 0)

    def send_rows(j):
        sends = to_rt(lambda t: routed.at[j, t], fs_ref.at[j, r], t2s.at[j], t2r.at[j])
        fs_ref[j, r] = routed[j, r]
        return sends

    def order(load, store, width):
        def split(n, carry):
            at = pl.ds(pl.multiple_of(n * LANES, LANES), LANES)
            rest = load(n)
            for p in range(3):
                piece = rest.astype(bf16)
                parts[p, at, :width] = piece
                rest = rest - piece.astype(f32)
            return carry

        lax.fori_loop(0, NR, split, 0)

        def rows_of(n, carry):
            at = pl.ds(pl.multiple_of(n * LANES, LANES), LANES)
            y = jnp.dot(perm[at, :], parts[0, :, :width], preferred_element_type=f32)
            y = y + jnp.dot(perm[at, :], parts[1, :, :width], preferred_element_type=f32)
            y = y + jnp.dot(perm[at, :], parts[2, :, :width], preferred_element_type=f32)
            store(at, y)
            return carry

        lax.fori_loop(0, ROWS_DEV // LANES, rows_of, 0)

    def order_columns(j, copies):
        wait_all(copies)

        def store(at, y):
            front_ref[at, j * QCOLS : (j + 1) * QCOLS] = y

        order(lambda n: fs_ref[j, n], store, QCOLS)

    def make_perm():
        def one(n, carry):
            at = pl.ds(pl.multiple_of(n * LANES, LANES), LANES)
            shape = (LANES, NR * NC * CAP)
            ids = lax.broadcasted_iota(jnp.int32, shape, 0) + n * LANES
            perm[at, :] = (jnp.broadcast_to(order_ref[0:1, :], shape) == ids).astype(f32).astype(bf16)
            return carry

        lax.fori_loop(0, ROWS_DEV // LANES, one, 0)

    panel = GatherCt(
        lambda h: pan_ref.at[pl.ds(h * SRC // 2, SRC // 2)],
        lambda h, o: ap.at[o, pl.ds(h * SRC // 2, SRC // 2)],
        r, c, a1s, a1r, a2s, a2r,
    )
    rows = GatherCt(
        lambda h: chunk.at[pl.ds(h * NR // 2, NR // 2)],
        lambda h, o: as_ref.at[pl.ds(h * NR // 2, NR // 2), o],
        r, c, c1s, c1r, c2s, c2r,
    )
    grams = GatherCt(
        lambda h: gsum.at[pl.ds(h * len(PAIRS) // 2, len(PAIRS) // 2)],
        lambda h, o: gbuf.at[o, pl.ds(h * len(PAIRS) // 2, len(PAIRS) // 2)],
        r, c, g1s, g1r, g2s, g2r,
    )

    def product(n, carry):
        i = n // QUARTERS
        j = lax.rem(n, QUARTERS)
        ah, al = two_parts(apt[pl.ds(pl.multiple_of(i * LANES, LANES), LANES), :])
        bh, bl = two_parts(fp[j].reshape(NC * SRC, QCOLS))
        y = jnp.dot(ah, bh, preferred_element_type=f32)
        y = y + jnp.dot(ah, bl, preferred_element_type=f32)
        y = y + jnp.dot(al, bh, preferred_element_type=f32)
        y = y.reshape(LANES // SLICE, SLICE, QCOLS)
        at = pl.ds(lax.rem(i, 2) * (LANES // SLICE), LANES // SLICE)
        part[i // 2, at, :, pl.ds(pl.multiple_of(j * QCOLS, QCOLS), QCOLS)] = y
        return carry

    columns = [start_columns(0)]
    panel.start()
    ap[c] = pan_ref[...]
    selections()
    po[...] = jnp.dot(
        sel_ref[c], three_parts(pan_ref[...]), preferred_element_type=f32
    ).reshape(NR, CAP, PANEL)
    chunks = to_rt(lambda t: po.at[t], chunk.at[r], p1s, p1r)
    chunk[r] = po[r]
    panel.forward()
    columns.append(start_columns(1))
    select_rows(0, columns[0])
    routes = [send_rows(0)]
    columns.append(start_columns(2))
    panel.finish()
    whole = ap[...].reshape(NC * SRC, PANEL)
    apt[...] = whole.T
    for i in range(PANEL // LANES):
        block = jnp.dot(
            apt[i * LANES : (i + 1) * LANES, :],
            ap[:, :, i * LANES :].reshape(NC * SRC, PANEL - i * LANES),
            precision=highest,
            preferred_element_type=f32,
        )
        for j in range(i, PANEL // LANES):
            piece = block[:, (j - i) * LANES : (j - i + 1) * LANES]
            gpart[:, PAIRS.index((i, j))] = piece.reshape(NC, SUB, LANES)
    gram_sends = to_rt(lambda t: gpart.at[c], gin.at[r], p3s, p3r)
    gin[r] = gpart[c]
    columns.append(start_columns(3))
    select_rows(1, columns[1])
    routes.append(send_rows(1))
    make_perm()
    wait_all(gram_sends)
    total = gin[0]
    for t in range(1, NR):
        total = total + gin[t]
    gsum[...] = total
    grams.start()
    gbuf[c] = total
    select_rows(2, columns[2])
    routes.append(send_rows(2))
    order_columns(0, routes[0])
    select_rows(3, columns[3])
    lax.fori_loop(0, QUARTERS * (PANEL // LANES), product, 0)
    swap = send(part.at[1 - core], ain, sa, ra, sibling, c)
    grams.forward()
    wait_all(chunks)
    rows.start()
    as_ref[:, c] = chunk[...]
    swap.wait()
    half[...] = part[core] + ain[...]
    spread = [
        send(half.at[peer // 2], bin_ref.at[d], sb.at[d], rb.at[d], peer, c)
        for d, peer in enumerate(chip_peers)
    ]
    order_columns(1, routes[1])
    grams.finish()
    for n, (i, j) in enumerate(PAIRS):
        work[i * LANES : (i + 1) * LANES, j * LANES : (j + 1) * LANES] = gbuf[:, n].reshape(LANES, LANES)
    ids = lax.broadcasted_iota(jnp.int32, (PANEL, PANEL), 0)
    lanes = lax.broadcasted_iota(jnp.int32, (PANEL, PANEL), 1)
    work[:, PANEL:] = jnp.where(ids == lanes, 1.0, 0.0).astype(f32)
    factor_step(0, work, small)
    factor_step(1, work, small)
    wait_all(spread)
    mine[...] = (half[x] + bin_ref[0]) + (bin_ref[1] + bin_ref[2])
    spread = [
        send(mine, full.at[core, x], sc.at[d], rc.at[d], peer, c) for d, peer in enumerate(chip_peers)
    ]
    last = [send(mine, full.at[core, x], sd.at[CHIPS - 1], rd.at[CHIPS - 1], sibling, c)]
    full[core, x] = mine[...]
    routes.append(send_rows(3))
    rows.forward()
    factor_step(2, work, small)
    for d, copy in enumerate(spread):
        copy.wait()
        owner = lax.rem(x + CHIPS - d - 1, CHIPS)
        last.append(
            send(full.at[core, owner], full.at[core, owner], sd.at[d], rd.at[d], sibling, c)
        )
    factor_step(3, work, small)
    inv_ref[...] = work[:, PANEL:]
    rows.finish()

    def store_rows(lane_at):
        def store(at, y):
            rows_ref[at, lane_at : lane_at + QCOLS] = y

        return store

    for n in range(PANEL // QCOLS):
        at = slice(n * QCOLS, (n + 1) * QCOLS)
        order(lambda t: as_ref[t].reshape(NC * CAP, PANEL)[:, at], store_rows(n * QCOLS), QCOLS)
    order_columns(2, routes[2])
    wait_all(last)
    sum_ref[...] = full[...].reshape(PANEL, BLOCK_COLS)
    order_columns(3, routes[3])


def factor_step(b, work, small):
    o = b * LANES
    lane = lax.broadcasted_iota(jnp.int32, (SUB, LANES), 1)
    sub = lax.broadcasted_iota(jnp.int32, (SUB, LANES), 0)
    block = [work[o + SUB * g : o + SUB * (g + 1), o : o + LANES] for g in range(LANES // SUB)]
    unit = [jnp.where(lane == sub + SUB * g, 1.0, 0.0).astype(f32) for g in range(LANES // SUB)]

    def write(g, v):
        small[SUB * g : SUB * (g + 1), :] = v

    inverse_of_block(block, unit, write)
    end = PANEL + o + LANES
    row = jnp.dot(
        small[...], work[o : o + LANES, o:end], precision=highest, preferred_element_type=f32
    )
    work[o : o + LANES, o:end] = row
    for p in range(o + LANES, PANEL, LANES):
        mult = row[:, p - o : p - o + LANES]
        work[p : p + LANES, p:end] = work[p : p + LANES, p:end] - jnp.dot(
            mult.T, row[:, p - o :], precision=highest, preferred_element_type=f32
        )


def build_front(columns, panel, slot, order):
    slots = NC * CAP
    vmem = pltpu.VMEM
    dma = pltpu.SemaphoreType.DMA
    n = len(PAIRS)
    ring = [dma((2, SIDE - 1)), dma((2, SIDE - 1)), dma((2, SIDE, SIDE - 1)), dma((2, SIDE, SIDE - 1))]
    return pl.pallas_call(
        front_kernel,
        in_specs=[pl.BlockSpec(memory_space=pltpu.VMEM)] * 4,
        out_specs=[pl.BlockSpec(memory_space=pltpu.VMEM)] * 4,
        out_shape=[
            jax.ShapeDtypeStruct((ROWS_DEV, BLOCK_COLS), f32),
            jax.ShapeDtypeStruct((ROWS_DEV, PANEL), f32),
            jax.ShapeDtypeStruct((PANEL, BLOCK_COLS), f32),
            jax.ShapeDtypeStruct((PANEL, PANEL), f32),
        ],
        scratch_shapes=[
            vmem((NC, NR * CAP, 3 * SRC), bf16),
            vmem((QUARTERS, NR, slots, QCOLS), f32),
            vmem((NR, NC, CAP, PANEL), f32),
            vmem((ROWS_DEV, NR * slots), bf16),
            vmem((3, NR * slots, QCOLS), bf16),
            vmem((NR, CAP, PANEL), f32),
            vmem((NR, CAP, PANEL), f32),
            vmem((NC, SRC, PANEL), f32),
            vmem((PANEL, NC * SRC), f32),
            vmem((NC, n, SUB, LANES), f32),
            vmem((NR, n, SUB, LANES), f32),
            vmem((n, SUB, LANES), f32),
            vmem((NC, n, SUB, LANES), f32),
            vmem((QUARTERS, NC, SRC, QCOLS), f32),
            vmem((QUARTERS, NR, slots, QCOLS), f32),
            vmem((PANEL, 2 * PANEL), f32),
            vmem((LANES, LANES), f32),
            vmem((2, CHIPS, SLICE, BLOCK_COLS), f32),
            vmem((CHIPS, SLICE, BLOCK_COLS), f32),
            vmem((CHIPS, SLICE, BLOCK_COLS), f32),
            vmem((CHIPS - 1, SLICE, BLOCK_COLS), f32),
            vmem((SLICE, BLOCK_COLS), f32),
            vmem((2, CHIPS, SLICE, BLOCK_COLS), f32),
            dma((NR - 1,)),
            dma((NR - 1,)),
            *ring,
            *ring,
            *ring,
            dma((NR - 1,)),
            dma((NR - 1,)),
            dma((QUARTERS, NC - 1)),
            dma((QUARTERS, NC - 1)),
            dma((QUARTERS, NR - 1)),
            dma((QUARTERS, NR - 1)),
            dma(()),
            dma(()),
            dma((CHIPS - 1,)),
            dma((CHIPS - 1,)),
            dma((CHIPS - 1,)),
            dma((CHIPS - 1,)),
            dma((CHIPS,)),
            dma((CHIPS,)),
        ],
        compiler_params=pltpu.CompilerParams(collective_id=0, has_side_effects=True),
        cost_estimate=pl.CostEstimate(
            flops=3_000_000_000, bytes_accessed=300_000_000, transcendentals=0
        ),
    )(columns, panel, slot, order)


def shards(children, row_map, column_map, staircase):
    placed = place_columns(children, row_map, column_map, staircase)
    front_block, panel_block, projected, inverse = build_front(*placed)
    basis = lax.dot_general(
        inverse, panel_block, (((1,), (1,)), ((), ())), precision=high, preferred_element_type=f32
    )
    factor_rows = jnp.dot(inverse, projected, precision=high, preferred_element_type=f32)
    update = lax.dot_general(
        basis, factor_rows, (((0,), (0,)), ((), ())), precision=high, preferred_element_type=f32
    )
    return (factor_rows, basis, front_block - update)


def solution(mesh):
    placed = (P(("rt", "ct"), None), P(), P(), P())
    return jax.shard_map(
        shards,
        mesh=mesh,
        in_specs=placed,
        out_specs=(P(None, "ct"), P(None, "rt"), P("rt", "ct")),
        check_vma=False,
    )
```

```python
import functools

import jax
import jax.numpy as jnp
from jax import lax
from jax.experimental import pallas as pl
from jax.experimental.pallas import tpu as pltpu
from jax.sharding import PartitionSpec as P

TILE = 256
PANEL = 512
SUB = 8
LANES = 128
NR = 8
NC = 16
SRC = 32
CAP = 8
ROWS_DEV = 512
BLOCK_COLS = 1024
FRONT_COLS = NC * BLOCK_COLS
FRONT_BLOCKS = FRONT_COLS // LANES
QUARTERS = 4
QCOLS = BLOCK_COLS // QUARTERS
SIDE = 4
COLUMN_ORDER = (1, 15, 4, 12, 5, 11, 3, 13, 8, 2, 14, 6, 10, 7, 9)
ROW_ORDER = (2, 6, 3, 5, 4, 7, 1)
CHIPS = NR // 2
SLICE = PANEL // NR
PAIRS = [(i, j) for i in range(PANEL // LANES) for j in range(i, PANEL // LANES)]

highest = lax.Precision.HIGHEST
high = lax.Precision.HIGH
f32 = jnp.float32
bf16 = jnp.bfloat16
MESH = pl.DeviceIdType.MESH


def table_kernel(
    stair_ref, row_ref, col_ref, ch_ref, x_ref, pan_ref, slot_ref, front_ref, code_ref, qv_ref, q_ref, sem
):
    r = lax.axis_index("rt")
    c = lax.axis_index("ct")
    child = r // (NR // 2)
    child_cols = col_ref.shape[1]
    rows = row_ref.shape[0]
    sub = lax.broadcasted_iota(jnp.int32, (LANES, LANES), 0)
    lane = lax.broadcasted_iota(jnp.int32, (LANES, LANES), 1)

    step = child_cols // 6
    ids = lax.broadcasted_iota(jnp.int32, (LANES, step), 0)
    present = jnp.zeros((LANES, LANES), f32)
    for n in range(6):
        cm = col_ref[pl.ds(child, 1), n * step : (n + 1) * step]
        cm = jnp.broadcast_to(cm, (LANES, step))
        upper = (jnp.right_shift(cm, 7) == ids).astype(f32).astype(bf16)
        lower = (jnp.bitwise_and(cm, LANES - 1) == ids).astype(f32).astype(bf16)
        present = present + lax.dot_general(
            upper, lower, (((1,), (1,)), ((), ())), preferred_element_type=f32
        )
    flags = present.astype(bf16)
    before = (sub < lane).astype(f32).astype(bf16)
    inside = jnp.dot(flags, before, preferred_element_type=f32)
    above = jnp.dot((lane < sub).astype(f32).astype(bf16), flags, preferred_element_type=f32)
    starts = jnp.sum(above, axis=1, keepdims=True).astype(jnp.int32)
    last = child_cols // LANES - 2
    q = jnp.minimum(jnp.right_shift(starts, 7), last)
    code = starts - q * LANES + inside.astype(jnp.int32)
    code_ref[...] = jnp.where(present > 0.5, code, -1)
    across = lax.dot_general(
        jnp.ones((SUB, LANES), bf16), above.astype(bf16), (((1,), (1,)), ((), ())),
        preferred_element_type=f32,
    )
    qv_ref[...] = jnp.minimum(jnp.right_shift(across.astype(jnp.int32), 7), last)

    rm = row_ref[...]
    tile = jnp.right_shift(rm, 9)
    group = jnp.right_shift(sub, 5) == jnp.right_shift(lane, 5)
    earlier = (group & (sub < lane)).astype(f32).astype(bf16)
    slot = jnp.zeros((rows, LANES), jnp.int32)
    for t in range(NR):
        hit = tile == t
        rank = jnp.dot(hit.astype(f32).astype(bf16), earlier, preferred_element_type=f32)
        slot = jnp.where(hit, t * CAP + rank.astype(jnp.int32), slot)
    slot_ref[...] = slot
    local = (rm - r * ROWS_DEV + 1).astype(f32)
    small_sub = lax.broadcasted_iota(jnp.int32, (LANES, SRC), 0)
    small_lane = lax.broadcasted_iota(jnp.int32, (LANES, SRC), 1)
    packed = jnp.zeros((rows, SRC), f32)
    for k in range(CAP):
        value = jnp.where(slot == r * CAP + k, local, 0.0)
        to = (jnp.right_shift(small_sub, 5) * CAP + k == small_lane).astype(f32)
        packed = packed + jnp.dot(value, to, precision=highest, preferred_element_type=f32)
    slots = NR * NC * CAP
    wide_sub = lax.broadcasted_iota(jnp.int32, (SRC, slots), 0)
    wide_lane = lax.broadcasted_iota(jnp.int32, (SRC, slots), 1)
    repeat = (jnp.bitwise_and(wide_lane, SRC - 1) == wide_sub).astype(f32)
    spread = jnp.dot(packed, repeat, precision=highest, preferred_element_type=f32)
    flat = jnp.where(jnp.right_shift(wide_lane, 5) == wide_sub, spread, 0.0)
    flat = jnp.sum(flat, axis=0, keepdims=True)
    front_ref[...] = jnp.broadcast_to(flat.astype(jnp.int32) - 1, (SUB, slots))
    fetch = pltpu.make_async_copy(qv_ref, q_ref, sem)
    fetch.start()

    first_row = lax.rem((r * NC + c) * SRC, NR * NC * SRC // 2)
    for t in range(PANEL // TILE):
        at = slice(t * TILE, (t + 1) * TILE)
        ids = lax.broadcasted_iota(jnp.int32, (SRC, TILE), 0)
        pan_ref[:, at] = jnp.where(ids + first_row < stair_ref[child, t], ch_ref[:, at], 0.0)
    fetch.wait()
    sub_ids = lax.broadcasted_iota(jnp.int32, (SUB, LANES), 0) + first_row
    halves = QCOLS // LANES

    def one(m, carry):
        j = m // (NC // 2)
        n = lax.rem(m, NC // 2)
        found = []
        for cc in range(2):
            for h in range(halves):
                b = (n * 2 + cc) * (BLOCK_COLS // LANES) + j * halves + h
                q = q_ref[0, b]
                start = pl.multiple_of(q * LANES, LANES)
                after = pl.multiple_of(start + LANES, LANES)
                code = jnp.broadcast_to(code_ref[pl.ds(b, 1), :], (SUB, LANES))
                lane = jnp.bitwise_and(code, LANES - 1)
                limit = jnp.where(
                    code < LANES,
                    stair_ref[child, q // (TILE // LANES)],
                    stair_ref[child, (q + 1) // (TILE // LANES)],
                )
                limit = jnp.where(code < 0, 0, limit)
                for g in range(SRC // SUB):
                    v0 = ch_ref[g * SUB : (g + 1) * SUB, pl.ds(start, LANES)]
                    v1 = ch_ref[g * SUB : (g + 1) * SUB, pl.ds(after, LANES)]
                    g0 = jnp.take_along_axis(v0, lane, axis=1)
                    g1 = jnp.take_along_axis(v1, lane, axis=1)
                    v = jnp.where(code < LANES, g0, g1)
                    found.append((cc, h, g, jnp.where(sub_ids + g * SUB < limit, v, 0.0)))
        for cc, h, g, v in found:
            x_ref[j, n * 2 + cc, g * SUB : (g + 1) * SUB, h * LANES : (h + 1) * LANES] = v
        return carry

    lax.fori_loop(0, QUARTERS * NC // 2, one, 0)


def place_columns(children, row_map, column_map, staircase):
    vmem = pl.BlockSpec(memory_space=pltpu.VMEM)
    rows = row_map.shape[0] // LANES
    return pl.pallas_call(
        table_kernel,
        in_specs=[pl.BlockSpec(memory_space=pltpu.SMEM)] + [vmem] * 3,
        out_specs=[vmem] * 4,
        out_shape=[
            jax.ShapeDtypeStruct((QUARTERS, NC, SRC, QCOLS), f32),
            jax.ShapeDtypeStruct((SRC, PANEL), f32),
            jax.ShapeDtypeStruct((rows, LANES), jnp.int32),
            jax.ShapeDtypeStruct((SUB, NR * NC * CAP), jnp.int32),
        ],
        scratch_shapes=[
            pltpu.VMEM((FRONT_BLOCKS, LANES), jnp.int32),
            pltpu.VMEM((SUB, FRONT_BLOCKS), jnp.int32),
            pltpu.SMEM((SUB, FRONT_BLOCKS), jnp.int32),
            pltpu.SemaphoreType.DMA,
        ],
        cost_estimate=pl.CostEstimate(flops=400_000_000, bytes_accessed=4_000_000, transcendentals=0),
    )(staircase, row_map.reshape(rows, LANES), column_map, children)


def across_lanes(v, lane):
    return jnp.broadcast_to(v[:, lane : lane + 1], (SUB, LANES))

def across_rows(v, row):
    return jnp.broadcast_to(v[row : row + 1, :], (SUB, LANES))

def inverse_of_block(block, unit, write):
    groups = LANES // SUB
    sub = lax.broadcasted_iota(jnp.int32, (SUB, LANES), 0)
    for g in range(groups):
        cols = [across_lanes(block[g], SUB * g + m) for m in range(SUB)]
        a = {(i, m): across_rows(cols[m], i) for m in range(SUB) for i in range(m, SUB)}
        low = {}
        inv = {}
        for k in range(SUB):
            inv[k, k] = lax.rsqrt(a[k, k])
            for i in range(k + 1, SUB):
                low[i, k] = a[i, k] * inv[k, k]
            for i in range(k + 1, SUB):
                for m in range(k + 1, i + 1):
                    a[i, m] = a[i, m] - low[i, k] * low[m, k]
        for i in range(1, SUB):
            for k in range(i):
                acc = low[i, k] * inv[k, k]
                for m in range(k + 1, i):
                    acc = acc + low[i, m] * inv[m, k]
                inv[i, k] = -inv[i, i] * acc
        zero = jnp.zeros((SUB, LANES), f32)
        down = []
        for k in range(SUB):
            col = zero
            for i in range(k, SUB):
                col = jnp.where(sub == i, inv[i, k], col)
            down.append(col)
        up = []
        for k in range(SUB):
            col = zero
            for i in range(k + 1):
                col = jnp.where(sub == i, inv[k, i], col)
            up.append(col)

        def apply(cols, v):
            terms = [cols[k] * across_rows(v, k) for k in range(SUB)]
            while len(terms) > 1:
                terms = [terms[i] + terms[i + 1] for i in range(0, len(terms), 2)]
            return terms[0]

        done = apply(down, unit[g])
        write(g, done)
        if g + 1 < groups:
            z = apply(up, apply(down, block[g]))
            zu = apply(up, done)
            zr = [across_rows(z, m) for m in range(SUB)]
            zur = [across_rows(zu, m) for m in range(SUB)]
            for i in range(g + 1, groups):
                mult = [across_lanes(block[i], SUB * g + m) for m in range(SUB)]
                t = [mult[m] * zr[m] for m in range(SUB)]
                u = [mult[m] * zur[m] for m in range(SUB)]
                while len(t) > 1:
                    t = [t[j] + t[j + 1] for j in range(0, len(t), 2)]
                    u = [u[j] + u[j + 1] for j in range(0, len(u), 2)]
                block[i] = block[i] - t[0]
                unit[i] = unit[i] - u[0]


def three_parts(x):
    hi = x.astype(bf16)
    rest = x - hi.astype(f32)
    mid = rest.astype(bf16)
    low = (rest - mid.astype(f32)).astype(bf16)
    return jnp.concatenate([hi, mid, low], axis=0)


def two_parts(x):
    hi = x.astype(bf16)
    return hi, (x - hi.astype(f32)).astype(bf16)


class GatherCt:
    def __init__(self, source, dest, r, c, s1, r1, s2, r2):
        self.source, self.dest, self.r, self.c = source, dest, r, c
        self.sems = (s1, r1, s2, r2)
        self.first, self.second = [], []

    def along(self, half, d):
        z, y = self.c // SIDE, lax.rem(self.c, SIDE)
        if half == 0:
            return z * SIDE + lax.rem(y + d, SIDE)
        return lax.rem(z + d, SIDE) * SIDE + y

    def send(self, src, half, owner, to, ss, rs):
        copy = pltpu.make_async_remote_copy(
            src_ref=src,
            dst_ref=self.dest(half, owner),
            send_sem=ss,
            recv_sem=rs,
            device_id=(self.r, to),
            device_id_type=MESH,
        )
        copy.start()
        return copy

    def start(self):
        s1, r1, s2, r2 = self.sems
        for d in range(1, SIDE):
            for h in range(2):
                to = self.along(h, d)
                copy = self.send(self.source(h), h, self.c, to, s1.at[h, d - 1], r1.at[h, d - 1])
                self.first.append(copy)
        for d in range(1, SIDE):
            for h in range(2):
                to = self.along(1 - h, d)
                copy = self.send(
                    self.source(h), h, self.c, to, s2.at[h, 0, d - 1], r2.at[h, 0, d - 1]
                )
                self.second.append(copy)

    def forward(self):
        s1, r1, s2, r2 = self.sems
        position = 0
        for p in range(1, SIDE):
            for h in range(2):
                self.first[position].wait()
                position += 1
                owner = self.along(h, SIDE - p)
                for d in range(1, SIDE):
                    to = self.along(1 - h, d)
                    copy = self.send(
                        self.dest(h, owner), h, owner, to, s2.at[h, p, d - 1], r2.at[h, p, d - 1]
                    )
                    self.second.append(copy)

    def finish(self):
        for copy in self.second:
            copy.wait()


def front_kernel(
    x_ref, pan_ref, slot_ref, order_ref,
    front_ref, rows_ref, sum_ref, inv_ref,
    sel_ref, fs_ref, as_ref, perm, parts, po, chunk, ap, apt, gpart, gin, gsum, gbuf, fp, routed, work, small,
    part, ain, half, bin_ref, mine, full,
    p1s, p1r, a1s, a1r, a2s, a2r, c1s, c1r, c2s, c2r, g1s, g1r, g2s, g2r, p3s, p3r,
    t1s, t1r, t2s, t2r, sa, ra, sb, rb, sc, rc, sd, rd,
):
    r = lax.axis_index("rt")
    c = lax.axis_index("ct")
    core = lax.rem(r, 2)
    x = r // 2
    sibling = r + 1 - 2 * core
    chip_peers = [2 * lax.rem(x + d, CHIPS) + core for d in range(1, CHIPS)]
    barrier = pltpu.get_barrier_semaphore()
    for d in range(1, NR):
        pl.semaphore_signal(barrier, inc=1, device_id=(lax.rem(r + d, NR), c), device_id_type=MESH)
    for e in range(1, NC):
        pl.semaphore_signal(barrier, inc=1, device_id=(r, lax.rem(c + e, NC)), device_id_type=MESH)

    pl.semaphore_wait(barrier, NR + NC - 2)

    def send(src, dst, ss, rs, rt, ct):
        copy = pltpu.make_async_remote_copy(
            src_ref=src, dst_ref=dst, send_sem=ss, recv_sem=rs, device_id=(rt, ct), device_id_type=MESH
        )
        copy.start()
        return copy

    def to_rt(src_of, dst, ss, rs):
        copies = []
        for d in ROW_ORDER:
            t = lax.rem(r + d, NR)
            copies.append(send(src_of(t), dst, ss.at[d - 1], rs.at[d - 1], t, c))
        return copies

    def wait_all(copies):
        for copy in copies:
            copy.wait()

    def selections():
        lane = lax.broadcasted_iota(jnp.int32, (NR * CAP, LANES), 1)
        ids = lax.broadcasted_iota(jnp.int32, (NR * CAP, LANES), 0)
        per = LANES // SRC
        for u in range(NC // per):
            row = jnp.broadcast_to(slot_ref[pl.ds(r * (NC // per) + u, 1), :], (NR * CAP, LANES))
            for v in range(per):
                turned = [
                    pltpu.roll(row, (g - v) % per * SRC, 1) if g != v else row for g in range(3)
                ]
                slots = jnp.where(lane < SRC, turned[0], jnp.where(lane < 2 * SRC, turned[1], turned[2]))
                chosen = (slots == ids).astype(f32).astype(bf16)
                sel_ref[u * per + v] = chosen[:, : 3 * SRC]

    def start_columns(j):
        copies = []
        for e in COLUMN_ORDER:
            to = lax.rem(c + e, NC)
            copies.append(
                send(x_ref.at[j, to], fp.at[j, c], t1s.at[j, e - 1], t1r.at[j, e - 1], r, to)
            )
        fp[j, c] = x_ref[j, c]
        return copies

    def select_rows(j, copies):
        wait_all(copies)

        def four(n, carry):
            done = []
            for i in range(4):
                s = n * 4 + i
                y = jnp.dot(sel_ref[s], three_parts(fp[j, s]), preferred_element_type=f32)
                done.append((s, y))
            for s, y in done:
                at = pl.ds(pl.multiple_of(s * CAP, CAP), CAP)
                routed[j, :, at, :] = y.reshape(NR, CAP, QCOLS)
            return carry

        lax.fori_loop(0, NC // 4, four, 0)

    def send_rows(j):
        sends = to_rt(lambda t: routed.at[j, t], fs_ref.at[j, r], t2s.at[j], t2r.at[j])
        fs_ref[j, r] = routed[j, r]
        return sends

    def order(load, store, width):
        def split(n, carry):
            at = pl.ds(pl.multiple_of(n * LANES, LANES), LANES)
            rest = load(n)
            hi, lo = two_parts(rest)
            parts[0, at, :width] = hi
            parts[1, at, :width] = lo
            return carry

        lax.fori_loop(0, NR, split, 0)

        def rows_of(n, carry):
            at = pl.ds(pl.multiple_of(n * LANES, LANES), LANES)
            y = jnp.dot(perm[at, :], parts[0, :, :width], preferred_element_type=f32)
            y = y + jnp.dot(perm[at, :], parts[1, :, :width], preferred_element_type=f32)
            store(at, y)
            return carry

        lax.fori_loop(0, ROWS_DEV // LANES, rows_of, 0)

    def order_columns(j, copies):
        wait_all(copies)

        def store(at, y):
            front_ref[at, j * QCOLS : (j + 1) * QCOLS] = y

        order(lambda n: fs_ref[j, n], store, QCOLS)

    def make_perm():
        def one(n, carry):
            at = pl.ds(pl.multiple_of(n * LANES, LANES), LANES)
            shape = (LANES, NR * NC * CAP)
            ids = lax.broadcasted_iota(jnp.int32, shape, 0) + n * LANES
            perm[at, :] = (jnp.broadcast_to(order_ref[0:1, :], shape) == ids).astype(f32).astype(bf16)
            return carry

        lax.fori_loop(0, ROWS_DEV // LANES, one, 0)

    panel = GatherCt(
        lambda h: pan_ref.at[pl.ds(h * SRC // 2, SRC // 2)],
        lambda h, o: ap.at[o, pl.ds(h * SRC // 2, SRC // 2)],
        r, c, a1s, a1r, a2s, a2r,
    )
    rows = GatherCt(
        lambda h: chunk.at[pl.ds(h * NR // 2, NR // 2)],
        lambda h, o: as_ref.at[pl.ds(h * NR // 2, NR // 2), o],
        r, c, c1s, c1r, c2s, c2r,
    )
    grams = GatherCt(
        lambda h: gsum.at[pl.ds(h * len(PAIRS) // 2, len(PAIRS) // 2)],
        lambda h, o: gbuf.at[o, pl.ds(h * len(PAIRS) // 2, len(PAIRS) // 2)],
        r, c, g1s, g1r, g2s, g2r,
    )

    def product(n, carry):
        i = n // QUARTERS
        j = lax.rem(n, QUARTERS)
        ah, al = two_parts(apt[pl.ds(pl.multiple_of(i * LANES, LANES), LANES), :])
        bh, bl = two_parts(fp[j].reshape(NC * SRC, QCOLS))
        y = jnp.dot(ah, bh, preferred_element_type=f32)
        y = y + jnp.dot(ah, bl, preferred_element_type=f32)
        y = y + jnp.dot(al, bh, preferred_element_type=f32)
        y = y.reshape(LANES // SLICE, SLICE, QCOLS)
        at = pl.ds(lax.rem(i, 2) * (LANES // SLICE), LANES // SLICE)
        part[i // 2, at, :, pl.ds(pl.multiple_of(j * QCOLS, QCOLS), QCOLS)] = y
        return carry

    columns = [start_columns(0)]
    panel.start()
    ap[c] = pan_ref[...]
    selections()
    po[...] = jnp.dot(
        sel_ref[c], three_parts(pan_ref[...]), preferred_element_type=f32
    ).reshape(NR, CAP, PANEL)
    chunks = to_rt(lambda t: po.at[t], chunk.at[r], p1s, p1r)
    chunk[r] = po[r]
    panel.forward()
    columns.append(start_columns(1))
    select_rows(0, columns[0])
    routes = [send_rows(0)]
    columns.append(start_columns(2))
    panel.finish()
    whole = ap[...].reshape(NC * SRC, PANEL)
    apt[...] = whole.T
    for i in range(PANEL // LANES):
        block = jnp.dot(
            apt[i * LANES : (i + 1) * LANES, :],
            ap[:, :, i * LANES :].reshape(NC * SRC, PANEL - i * LANES),
            precision=highest,
            preferred_element_type=f32,
        )
        for j in range(i, PANEL // LANES):
            piece = block[:, (j - i) * LANES : (j - i + 1) * LANES]
            gpart[:, PAIRS.index((i, j))] = piece.reshape(NC, SUB, LANES)
    gram_sends = to_rt(lambda t: gpart.at[c], gin.at[r], p3s, p3r)
    gin[r] = gpart[c]
    columns.append(start_columns(3))
    select_rows(1, columns[1])
    routes.append(send_rows(1))
    make_perm()
    wait_all(gram_sends)
    total = gin[0]
    for t in range(1, NR):
        total = total + gin[t]
    gsum[...] = total
    grams.start()
    gbuf[c] = total
    select_rows(2, columns[2])
    routes.append(send_rows(2))
    order_columns(0, routes[0])
    select_rows(3, columns[3])
    lax.fori_loop(0, QUARTERS * (PANEL // LANES), product, 0)
    swap = send(part.at[1 - core], ain, sa, ra, sibling, c)
    grams.forward()
    wait_all(chunks)
    rows.start()
    as_ref[:, c] = chunk[...]
    swap.wait()
    half[...] = part[core] + ain[...]
    spread = [
        send(half.at[peer // 2], bin_ref.at[d], sb.at[d], rb.at[d], peer, c)
        for d, peer in enumerate(chip_peers)
    ]
    order_columns(1, routes[1])
    grams.finish()
    for n, (i, j) in enumerate(PAIRS):
        work[i * LANES : (i + 1) * LANES, j * LANES : (j + 1) * LANES] = gbuf[:, n].reshape(LANES, LANES)
    ids = lax.broadcasted_iota(jnp.int32, (PANEL, PANEL), 0)
    lanes = lax.broadcasted_iota(jnp.int32, (PANEL, PANEL), 1)
    work[:, PANEL:] = jnp.where(ids == lanes, 1.0, 0.0).astype(f32)
    factor_step(0, work, small)
    factor_step(1, work, small)
    wait_all(spread)
    mine[...] = (half[x] + bin_ref[0]) + (bin_ref[1] + bin_ref[2])
    spread = [
        send(mine, full.at[core, x], sc.at[d], rc.at[d], peer, c) for d, peer in enumerate(chip_peers)
    ]
    last = [send(mine, full.at[core, x], sd.at[CHIPS - 1], rd.at[CHIPS - 1], sibling, c)]
    full[core, x] = mine[...]
    routes.append(send_rows(3))
    rows.forward()
    factor_step(2, work, small)
    for d, copy in enumerate(spread):
        copy.wait()
        owner = lax.rem(x + CHIPS - d - 1, CHIPS)
        last.append(
            send(full.at[core, owner], full.at[core, owner], sd.at[d], rd.at[d], sibling, c)
        )
    factor_step(3, work, small)
    inv_ref[...] = work[:, PANEL:]
    rows.finish()

    def store_rows(lane_at):
        def store(at, y):
            rows_ref[at, lane_at : lane_at + QCOLS] = y

        return store

    for n in range(PANEL // QCOLS):
        at = slice(n * QCOLS, (n + 1) * QCOLS)
        order(lambda t: as_ref[t].reshape(NC * CAP, PANEL)[:, at], store_rows(n * QCOLS), QCOLS)
    order_columns(2, routes[2])
    wait_all(last)
    sum_ref[...] = full[...].reshape(PANEL, BLOCK_COLS)
    order_columns(3, routes[3])


def factor_step(b, work, small):
    o = b * LANES
    lane = lax.broadcasted_iota(jnp.int32, (SUB, LANES), 1)
    sub = lax.broadcasted_iota(jnp.int32, (SUB, LANES), 0)
    block = [work[o + SUB * g : o + SUB * (g + 1), o : o + LANES] for g in range(LANES // SUB)]
    unit = [jnp.where(lane == sub + SUB * g, 1.0, 0.0).astype(f32) for g in range(LANES // SUB)]

    def write(g, v):
        small[SUB * g : SUB * (g + 1), :] = v

    inverse_of_block(block, unit, write)
    end = PANEL + o + LANES
    row = jnp.dot(
        small[...], work[o : o + LANES, o:end], precision=highest, preferred_element_type=f32
    )
    work[o : o + LANES, o:end] = row
    for p in range(o + LANES, PANEL, LANES):
        mult = row[:, p - o : p - o + LANES]
        work[p : p + LANES, p:end] = work[p : p + LANES, p:end] - jnp.dot(
            mult.T, row[:, p - o :], precision=highest, preferred_element_type=f32
        )


def build_front(columns, panel, slot, order):
    slots = NC * CAP
    vmem = pltpu.VMEM
    dma = pltpu.SemaphoreType.DMA
    n = len(PAIRS)
    ring = [dma((2, SIDE - 1)), dma((2, SIDE - 1)), dma((2, SIDE, SIDE - 1)), dma((2, SIDE, SIDE - 1))]
    return pl.pallas_call(
        front_kernel,
        in_specs=[pl.BlockSpec(memory_space=pltpu.VMEM)] * 4,
        out_specs=[pl.BlockSpec(memory_space=pltpu.VMEM)] * 4,
        out_shape=[
            jax.ShapeDtypeStruct((ROWS_DEV, BLOCK_COLS), f32),
            jax.ShapeDtypeStruct((ROWS_DEV, PANEL), f32),
            jax.ShapeDtypeStruct((PANEL, BLOCK_COLS), f32),
            jax.ShapeDtypeStruct((PANEL, PANEL), f32),
        ],
        scratch_shapes=[
            vmem((NC, NR * CAP, 3 * SRC), bf16),
            vmem((QUARTERS, NR, slots, QCOLS), f32),
            vmem((NR, NC, CAP, PANEL), f32),
            vmem((ROWS_DEV, NR * slots), bf16),
            vmem((2, NR * slots, QCOLS), bf16),
            vmem((NR, CAP, PANEL), f32),
            vmem((NR, CAP, PANEL), f32),
            vmem((NC, SRC, PANEL), f32),
            vmem((PANEL, NC * SRC), f32),
            vmem((NC, n, SUB, LANES), f32),
            vmem((NR, n, SUB, LANES), f32),
            vmem((n, SUB, LANES), f32),
            vmem((NC, n, SUB, LANES), f32),
            vmem((QUARTERS, NC, SRC, QCOLS), f32),
            vmem((QUARTERS, NR, slots, QCOLS), f32),
            vmem((PANEL, 2 * PANEL), f32),
            vmem((LANES, LANES), f32),
            vmem((2, CHIPS, SLICE, BLOCK_COLS), f32),
            vmem((CHIPS, SLICE, BLOCK_COLS), f32),
            vmem((CHIPS, SLICE, BLOCK_COLS), f32),
            vmem((CHIPS - 1, SLICE, BLOCK_COLS), f32),
            vmem((SLICE, BLOCK_COLS), f32),
            vmem((2, CHIPS, SLICE, BLOCK_COLS), f32),
            dma((NR - 1,)),
            dma((NR - 1,)),
            *ring,
            *ring,
            *ring,
            dma((NR - 1,)),
            dma((NR - 1,)),
            dma((QUARTERS, NC - 1)),
            dma((QUARTERS, NC - 1)),
            dma((QUARTERS, NR - 1)),
            dma((QUARTERS, NR - 1)),
            dma(()),
            dma(()),
            dma((CHIPS - 1,)),
            dma((CHIPS - 1,)),
            dma((CHIPS - 1,)),
            dma((CHIPS - 1,)),
            dma((CHIPS,)),
            dma((CHIPS,)),
        ],
        compiler_params=pltpu.CompilerParams(collective_id=0, has_side_effects=True),
        cost_estimate=pl.CostEstimate(
            flops=3_000_000_000, bytes_accessed=300_000_000, transcendentals=0
        ),
    )(columns, panel, slot, order)


def shards(children, row_map, column_map, staircase):
    placed = place_columns(children, row_map, column_map, staircase)
    front_block, panel_block, projected, inverse = build_front(*placed)
    basis = lax.dot_general(
        inverse, panel_block, (((1,), (1,)), ((), ())), precision=high, preferred_element_type=f32
    )
    factor_rows = jnp.dot(inverse, projected, precision=high, preferred_element_type=f32)
    update = lax.dot_general(
        basis, factor_rows, (((0,), (0,)), ((), ())), precision=high, preferred_element_type=f32
    )
    return (factor_rows, basis, front_block - update)


def solution(mesh):
    placed = (P(("rt", "ct"), None), P(), P(), P())
    return jax.shard_map(
        shards,
        mesh=mesh,
        in_specs=placed,
        out_specs=(P(None, "ct"), P(None, "rt"), P("rt", "ct")),
        check_vma=False,
    )
```
